256 devices in a mesh: row: 8 (over y, core), col: 16 (over z, x_hi), wave: 2 (over x_lo).
Axes of the slice: x: 4 (x_hi: 2, x_lo: 2; x = x_hi * 2 + x_lo), y: 4, z: 8, core: 2. Of those that a mesh axis runs over, the one named last changes fastest.
Arguments:
- lower_panel: float32 [16, 64, 4096], P('wave', None, 'col'), may hold values from -1.5 to 1.5
- diag_inverse: float32 [16, 64, 64], P('wave'), may hold values from -0.75 to 0.75
- ancestor_inverse: float32 [16384, 16384], P('row', ('col', 'wave')), may hold values from -0.1875 to 0.1875
- pattern: int32 [16, 32], P('wave'), may hold values from 0 to 127, as said below
Outputs:
- inverse_panel: float32 [16, 64, 16384], P('wave', None, ('row', 'col'))
- diag_block: float32 [16, 64, 64], P('wave')
The draws below stay inside these ranges and needn't reach their ends.
Inputs may be any that keep to these rules, and one draw needn't show every extreme that they name: `pattern`: each row holds 32 different block numbers in rising order, and every row includes 0, 127 and half of 128.
All inputs are finite; a program needn't handle non-finite values.
Results may differ from the reference program's by a relative error of at most 0.000096.
Values sent between devices are 32-bit elements; how exact they have to be, the bound alone decides.
A program may use at most 128 MiB of HBM per device.

```python
import jax
import jax.numpy as jnp
from jax import lax

W = 64
BLK = 128
SIBS = 16
ANCESTOR_BLOCKS = 128
NBK = 32
R = 16384


def shuffled(key_one):
    return jax.random.permutation(key_one, ANCESTOR_BLOCKS).astype(jnp.int32)


def draw_pattern(key, part):
    key_perm = jax.random.fold_in(key, 11)
    group_key = jax.random.fold_in(key, 12)
    extra_score_group = jax.random.randint(group_key, (ANCESTOR_BLOCKS // 8,), 0, 4).astype(jnp.int32)
    extra_score_full = jnp.repeat(extra_score_group, 8)
    key_list = jax.random.split(key_perm, SIBS)
    block_orders = jax.vmap(shuffled)(key_list)
    blocks = jnp.arange(ANCESTOR_BLOCKS, dtype=jnp.int32)
    needed = (blocks == 0) | (blocks == ANCESTOR_BLOCKS - 1) | (blocks == ANCESTOR_BLOCKS // 2)
    required_choice = jnp.where(needed, 8, 0).astype(jnp.int32)
    block_scores = (extra_score_full + required_choice)[None, :] * ANCESTOR_BLOCKS + block_orders
    values_top, chosen = lax.top_k(block_scores, NBK)
    return jnp.sort(chosen, axis=1).astype(jnp.int32)


def raised(drawn, stream_key, source, target, parts, factor):
    owner, partner = [(jnp.arange(drawn.shape[dim]) // (drawn.shape[dim] // parts)).reshape([-1 if axis == dim else 1 for axis in range(drawn.ndim)]) for dim in (source, target)]
    chosen = jax.random.permutation(stream_key, parts)[partner]
    strong = (owner == chosen) | (owner == (partner + parts // 2) % parts)
    return jnp.where(strong, factor * drawn, drawn)


def shard_levels(own_key, dims, cuts, least, high):
    loudness = 1.0
    for dim, blocks in cuts:
        draws = jax.random.uniform(jax.random.fold_in(jax.random.fold_in(own_key, 6), dim), (blocks,), jnp.float32, least / len(cuts), high / len(cuts))
        loudness = loudness * jnp.repeat(jnp.exp(draws), dims[dim] // blocks).reshape((-1,) + (1,) * (len(dims) - 1 - dim))
    return loudness


def gaussian(rng, shape, width, limit, cuts=(), kind=jnp.bfloat16):
    loudness = shard_levels(rng, shape, cuts, -0.22, 0.18) if cuts else 1.0
    entries = jax.random.normal(rng, shape, jnp.float32) * width * loudness
    return jnp.minimum(jnp.maximum(entries, -limit), limit).astype(kind)


def bell_draw_with(own_key, shape, width, most, cuts, heavy, held_as=jnp.bfloat16):
    result = width * jax.random.normal(own_key, shape, jnp.float32)
    if cuts:
        result = result * shard_levels(own_key, shape, cuts, -0.22, 0.18)
    return jnp.clip(raised(result, jax.random.fold_in(own_key, 3), *heavy), -most, most).astype(held_as)


def setup_inputs(seed: int = 0) -> dict:
    arg_keys = jax.random.split(jax.random.key(seed), 5)
    lower_panel = gaussian(arg_keys[0], (SIBS, W, NBK * BLK), 0.25, 1.5, ((0, 2), (2, 16)), jnp.float32)
    diag_inverse = gaussian(arg_keys[1], (SIBS, W, W), W ** -0.5, 0.75, ((0, 2),), jnp.float32)
    ancestor_inverse = bell_draw_with(arg_keys[2], (R, R), (NBK * BLK) ** -0.5, 0.1875, ((0, 8), (1, 32)), (1, 0, 32, 2.75), jnp.float32)
    pattern = draw_pattern(jax.random.fold_in(arg_keys[4], 71), 0)
    return {"lower_panel": lower_panel, "diag_inverse": diag_inverse, "ancestor_inverse": ancestor_inverse, "pattern": pattern}


def reference(lower_panel, diag_inverse, ancestor_inverse, pattern):
    highest = lax.Precision.HIGHEST
    normed = jnp.einsum("svw,svk->swk", diag_inverse, lower_panel, precision=highest)
    packed = normed.reshape(SIBS, W, NBK, BLK)
    blocks = jnp.arange(ANCESTOR_BLOCKS, dtype=jnp.int32)
    onehot = (pattern[:, None, :] == blocks[None, :, None]).astype(jnp.float32)
    dense_panel = jnp.einsum("sqk,swkb->swqb", onehot, packed, precision=highest).reshape(SIBS * W, ANCESTOR_BLOCKS * BLK)
    product = lax.dot_general(dense_panel, ancestor_inverse, (((1,), (1,)), ((), ())), precision=highest)
    row_mask = jnp.repeat(jnp.sum(onehot, axis=2), BLK, axis=1)
    inverse_panel = -product.reshape(SIBS, W, ANCESTOR_BLOCKS * BLK) * row_mask[:, None, :]
    base_block = jnp.einsum("svw,svx->swx", diag_inverse, diag_inverse, precision=highest)
    update = jnp.einsum("swr,sxr->swx", dense_panel.reshape(SIBS, W, ANCESTOR_BLOCKS * BLK), inverse_panel, precision=highest)
    return inverse_panel, base_block - update
```

```python
import jax
import jax.numpy as jnp
from jax import lax
from jax.experimental import pallas as pl
from jax.experimental.pallas import tpu as pltpu
from jax.sharding import Mesh
from jax.sharding import PartitionSpec as P

W = 64
BLK = 128
Y, CORES, Z, XH, WAVES = 4, 2, 8, 2, 2
ROWS = Y * CORES
COLS = Z * XH
KCOLS = 1024
HALF = KCOLS // 2
COL = ("col_0", "col_1")
ROW = ("row_0", "row_1")
ROW_COL = ("row_0", "row_1", "col_0", "col_1")
COL_WAVE = ("col_0", "col_1", "wave")
MESH = pl.DeviceIdType.MESH
HIGHEST = lax.Precision.HIGHEST
F32 = jnp.float32
BF16 = jnp.bfloat16


def remote(src, dst, send, recv, **device):
    return pltpu.make_async_remote_copy(
        src_ref=src,
        dst_ref=dst,
        send_sem=send,
        recv_sem=recv,
        device_id=device,
        device_id_type=MESH,
    )


def halves(value):
    high = value.astype(BF16)
    return high, (value - high.astype(F32)).astype(BF16)


def dot_last(left, right, precision=None):
    return lax.dot_general(
        left, right, (((1,), (1,)), ((), ())), precision=precision, preferred_element_type=F32
    )


def dot_first(left, right):
    return lax.dot_general(
        left, right, (((0,), (0,)), ((), ())), precision=HIGHEST, preferred_element_type=F32
    )


def kernel(
    table,
    lower,
    diag,
    ancestor,
    panel_out,
    block_out,
    packed,
    dense,
    dense_hi,
    dense_lo,
    abuf,
    a_hi,
    a_lo,
    part,
    ring_in,
    summed,
    cross_in,
    row_blocks,
    own_rows,
    update,
    row_in,
    col_part,
    col_in,
    total,
    a_send,
    a_recv,
    a_loc,
    h_sem,
    zp_send,
    zp_recv,
    zm_send,
    zm_recv,
    w_sem,
    y_send,
    y_recv,
    f_send,
    f_recv,
    c_send,
    c_recv,
    b_send,
    b_recv,
    r_send,
    r_recv,
    x_send,
    x_recv,
    u_send,
    u_recv,
    v_send,
    v_recv,
    t_send,
    t_recv,
):
    y = lax.axis_index("row_0")
    k = lax.axis_index("row_1")
    z = lax.axis_index("col_0")
    h = lax.axis_index("col_1")
    w = lax.axis_index("wave")
    r = y * CORES + k
    c = z * XH + h

    def row_peer(offset):
        other = (r + offset) % ROWS
        return other, {"row_0": other // CORES, "row_1": other % CORES}

    def col_peer(offset):
        other = (c + offset) % COLS
        return other, {"col_0": other // XH, "col_1": other % XH}

    barrier = pltpu.get_barrier_semaphore()

    def greet(device):
        pl.semaphore_signal(barrier, inc=1, device_id=device, device_id_type=MESH)

    greet({"wave": 1 - w})
    greet({"col_1": 1 - h, "wave": 1 - w})
    for offset in range(1, ROWS):
        greet(row_peer(offset)[1])
    for offset in range(1, COLS):
        greet(col_peer(offset)[1])

    local = [
        pltpu.make_async_copy(ancestor.at[d, w], abuf.at[d, w], a_loc.at[d]) for d in range(Z)
    ]
    for copy in local:
        copy.start()
    normed = dot_first(diag[r], lower[r])
    slot = 2 * c
    packed[slot] = normed[:, :BLK]
    packed[slot + 1] = normed[:, BLK:]

    pl.semaphore_wait(barrier, 2 + (ROWS - 1) + (COLS - 1))

    def pair_at(place, side):
        return packed.at[pl.ds(2 * (place * XH + side), 2)]

    trade = remote(pair_at(z, h), pair_at(z, h), h_sem.at[0], h_sem.at[1], col_1=1 - h)
    trade.start()

    a_copies = [
        remote(
            ancestor.at[d, 1 - w], abuf.at[d, w], a_send.at[d], a_recv.at[d], wave=1 - w
        )
        for d in range(Z)
    ]
    z_up, z_down = (z + 1) % Z, (z + Z - 1) % Z

    def z_gather(step, own, up):
        side = h if own == 0 else 1 - h
        source = (z + Z - (step - 1)) % Z if up else (z + step - 1) % Z
        if step < 4:
            view = pair_at(source, side)
        else:
            view = packed.at[pl.ds(2 * (source * XH + side) + (0 if up else 1), 1)]
        send, recv = (zp_send, zp_recv) if up else (zm_send, zm_recv)
        slot_id = 2 * (step - 1) + own
        return remote(
            view, view, send.at[slot_id], recv.at[slot_id], col_0=z_up if up else z_down
        )

    gathers = {}
    for step in range(1, 5):
        for own in range(2):
            if step == 1 and own == 1:
                trade.wait_recv()
            for up in (True, False):
                if step > 1:
                    gathers[step - 1, own, up].wait_recv()
                copy = z_gather(step, own, up)
                copy.start()
                gathers[step, own, up] = copy
        if step <= 3:
            a_copies[step - 1].start()
    for own in range(2):
        for up in (True, False):
            gathers[4, own, up].wait_recv()

    def placed(block):
        found = table[r, block]
        value = packed[jnp.maximum(found - 1, 0)]
        return jnp.where(found > 0, value, jnp.zeros_like(value))

    for j in range(8):
        dense[w, r, :, j * BLK : (j + 1) * BLK] = placed(8 * c + j)

    def spread(group, row, send, recv, **device):
        return remote(dense.at[group, row], dense.at[group, row], send, recv, **device)

    wave_copy = spread(w, r, w_sem.at[0], w_sem.at[1], wave=1 - w)
    wave_copy.start()
    for d in range(3, Z):
        a_copies[d].start()
    y_up, y_down = (y + 1) % Y, (y + Y - 1) % Y
    waves = (w, 1 - w)

    def y_copy(item, up):
        slot_id = 2 * item + (0 if up else 1)
        return spread(
            waves[item], r, y_send.at[slot_id], y_recv.at[slot_id], row_0=y_up if up else y_down
        )

    def core_copy(item, dy):
        row = ((y + dy) % Y) * CORES + k
        slot_id = 4 * item + dy
        return spread(waves[item], row, c_send.at[slot_id], c_recv.at[slot_id], row_1=1 - k)

    y_copies = {(item, up): y_copy(item, up) for item in range(2) for up in (True, False)}
    core_copies = {(item, dy): core_copy(item, dy) for item in range(2) for dy in range(Y)}
    far_up = spread(w, y_down * CORES + k, f_send.at[0], f_recv.at[0], row_0=y_up)
    far_down = spread(1 - w, y_up * CORES + k, f_send.at[1], f_recv.at[1], row_0=y_down)

    y_copies[0, True].start()
    y_copies[0, False].start()
    core_copies[0, 0].start()
    for row in range(ROWS):
        row_blocks[row] = placed(row * COLS + c)
    wave_copy.wait_recv()
    y_copies[1, True].start()
    y_copies[1, False].start()
    core_copies[1, 0].start()
    y_copies[0, True].wait_recv()
    far_up.start()
    core_copies[0, 3].start()
    y_copies[1, False].wait_recv()
    far_down.start()
    core_copies[1, 1].start()
    y_copies[0, False].wait_recv()
    core_copies[0, 1].start()
    y_copies[1, True].wait_recv()
    core_copies[1, 3].start()

    own_rows[r] = row_blocks[r]
    block_copies = []
    for offset in range(1, ROWS):
        other, device = row_peer(offset)
        copy = remote(
            row_blocks.at[other],
            own_rows.at[r],
            b_send.at[offset],
            b_recv.at[offset],
            **device,
        )
        copy.start()
        block_copies.append(copy)

    far_up.wait_recv()
    core_copies[0, 2].start()
    far_down.wait_recv()
    core_copies[1, 2].start()
    for copy in core_copies.values():
        copy.wait_recv()

    def split_dense(index, carry):
        rows = pl.ds(pl.multiple_of(index * W, W), W)
        high, low = halves(dense[index // ROWS, index % ROWS])
        dense_hi[rows, :] = high
        dense_lo[rows, :] = low
        return carry

    lax.fori_loop(0, WAVES * ROWS, split_dense, 0)
    for copy in local:
        copy.wait()
    for copy in a_copies:
        copy.wait_recv()

    def split_ancestor(index, carry):
        for side in range(WAVES):
            high, low = halves(abuf[index, side])
            a_hi[index, :, side * HALF : (side + 1) * HALF] = high
            a_lo[index, :, side * HALF : (side + 1) * HALF] = low
        return carry

    lax.fori_loop(0, Z, split_ancestor, 0)

    def multiply(index, carry):
        first = 2 * (index // 4)
        rows = pl.ds(pl.multiple_of((index % 4) * 256, 256), 256)
        right_hi = a_hi[pl.ds(first, 2)].reshape(2 * BLK, KCOLS)
        right_lo = a_lo[pl.ds(first, 2)].reshape(2 * BLK, KCOLS)
        left_hi, left_lo = dense_hi[rows, :], dense_lo[rows, :]
        product = (
            dot_last(left_hi, right_lo) + dot_last(left_lo, right_hi)
        ) + dot_last(left_hi, right_hi)
        part[first, rows, :] = product[:, :BLK]
        part[first + 1, rows, :] = product[:, BLK:]
        return carry

    lax.fori_loop(0, 16, multiply, 0)

    def ring_place(t, sub):
        return (z + 2 * Z - 1 - t) % Z if sub < 2 else (z + 1 + t) % Z

    def ring_copy(t, sub):
        rows = pl.ds(sub * 256, 256)
        return remote(
            part.at[ring_place(t, sub), rows],
            ring_in.at[t, rows],
            r_send.at[sub, t],
            r_recv.at[sub, t],
            col_0=z_up if sub < 2 else z_down,
        )

    for sub in (0, 2, 1, 3):
        ring_copy(0, sub).start()

    def ring_step(t, carry):
        for sub in (0, 2, 1, 3):
            rows = pl.ds(sub * 256, 256)
            ring_copy(t - 1, sub).wait_recv()
            place = ring_place(t, sub)
            part[place, rows, :] = part[place, rows, :] + ring_in[t - 1, rows, :]
            ring_copy(t, sub).start()
        return carry

    lax.fori_loop(1, Z - 1, ring_step, 0)

    def cross_copy(sub):
        return remote(
            summed.at[pl.ds(sub * 256, 256)],
            cross_in.at[h, pl.ds((sub % 2) * 256, 256)],
            x_send.at[sub],
            x_recv.at[h, sub % 2],
            col_1=w,
            wave=sub // 2,
        )

    def stays(sub):
        return jnp.logical_and(h == w, w == sub // 2)

    for sub in (0, 2, 1, 3):
        rows = pl.ds(sub * 256, 256)
        ring_copy(Z - 2, sub).wait_recv()
        summed[rows, :] = part[z, rows, :] + ring_in[Z - 2, rows, :]

        @pl.when(jnp.logical_not(stays(sub)))
        def _():
            cross_copy(sub).start()

        @pl.when(stays(sub))
        def _():
            cross_in[h, pl.ds((sub % 2) * 256, 256), :] = summed[rows, :]

    for copy in block_copies:
        copy.wait_recv()

    for piece in range(2):
        for side in range(XH):
            rows = pl.ds(piece * 256, 256)

            @pl.when(jnp.logical_not(jnp.logical_and(h == w, h == side)))
            def _():
                remote(
                    summed.at[rows],
                    cross_in.at[side, rows],
                    x_send.at[0],
                    x_recv.at[side, piece],
                    col_1=1 - h,
                ).wait_recv()

    for s in range(ROWS):
        rows = pl.ds(s * W, W)
        value = -(cross_in[0, rows, :] + cross_in[1, rows, :])
        found = table[s, r * COLS + c]
        value = jnp.where(found > 0, value, jnp.zeros_like(value))
        panel_out[s] = value
        lanes = slice((s % 2) * W, (s % 2 + 1) * W)
        update[s // 2, :, lanes] = dot_last(own_rows[s], value, HIGHEST)

    def share(row):
        return update.at[row // CORES, pl.ds((row % CORES) * 32, 32)]

    u_copies = []
    for offset in range(1, ROWS):
        other, device = row_peer(offset)
        copy = remote(
            share(other), row_in.at[offset], u_send.at[offset], u_recv.at[offset], **device
        )
        copy.start()
        u_copies.append(copy)
    partial = update[y, pl.ds(pl.multiple_of(k * 32, 32), 32), :]
    for offset in range(1, ROWS):
        u_copies[offset - 1].wait_recv()
        partial = partial + row_in[offset]
    col_part[...] = partial
    v_copies = []
    for offset in range(1, COLS):
        copy = remote(
            col_part, col_in.at[offset], v_send.at[offset], v_recv.at[offset], **col_peer(offset)[1]
        )
        copy.start()
        v_copies.append(copy)
    col_in[0] = col_part[...]
    for copy in v_copies:
        copy.wait_recv()
    whole = col_in[c]
    for owner in range(1, COLS):
        whole = whole + col_in[(c + COLS - owner) % COLS]
    mine = pl.ds(pl.multiple_of(k * 32, 32), 32)
    total[y, mine, :] = whole
    t_copies = []
    for offset in range(1, ROWS):
        copy = remote(
            total.at[y, mine],
            total.at[y, mine],
            t_send.at[offset],
            t_recv.at[offset],
            **row_peer(offset)[1],
        )
        copy.start()
        t_copies.append(copy)
    for copy in t_copies:
        copy.wait_recv()
    for s in range(ROWS):
        base = dot_first(diag[s], diag[s])
        lanes = slice((s % 2) * W, (s % 2 + 1) * W)
        block_out[s] = base - total[s // 2, :, lanes]

    trade.wait_send()
    for copy in gathers.values():
        copy.wait_send()
    for copy in a_copies:
        copy.wait_send()
    wave_copy.wait_send()
    for copy in y_copies.values():
        copy.wait_send()
    for copy in core_copies.values():
        copy.wait_send()
    far_up.wait_send()
    far_down.wait_send()
    for copy in block_copies + u_copies + v_copies + t_copies:
        copy.wait_send()

    def ring_sent(t, carry):
        for sub in range(4):
            ring_copy(t, sub).wait_send()
        return carry

    lax.fori_loop(0, Z - 1, ring_sent, 0)
    for sub in range(4):

        @pl.when(jnp.logical_not(stays(sub)))
        def _():
            cross_copy(sub).wait_send()


def per_device(lower_panel, diag_inverse, ancestor_inverse, pattern):
    blocks = jnp.arange(R_BLOCKS, dtype=jnp.int32)
    places = jnp.arange(1, pattern.shape[1] + 1, dtype=jnp.int32)
    hits = pattern[:, None, :] == blocks[None, :, None]
    table = jnp.max(jnp.where(hits, places[None, None, :], 0), axis=2)
    ancestor = ancestor_inverse.reshape(Z, XH, BLK, HALF)
    vmem = pl.BlockSpec(memory_space=pltpu.VMEM)
    dma = pltpu.SemaphoreType.DMA
    return pl.pallas_call(
        kernel,
        out_shape=(
            jax.ShapeDtypeStruct((ROWS, W, BLK), F32),
            jax.ShapeDtypeStruct((ROWS, W, W), F32),
        ),
        in_specs=[
            pl.BlockSpec(memory_space=pltpu.SMEM),
            vmem,
            vmem,
            pl.BlockSpec(memory_space=pl.ANY),
        ],
        out_specs=(vmem, vmem),
        scratch_shapes=[
            pltpu.VMEM((32, W, BLK), F32),
            pltpu.VMEM((WAVES, ROWS, W, KCOLS), F32),
            pltpu.VMEM((WAVES * ROWS * W, KCOLS), BF16),
            pltpu.VMEM((WAVES * ROWS * W, KCOLS), BF16),
            pltpu.VMEM((Z, WAVES, BLK, HALF), F32),
            pltpu.VMEM((Z, BLK, KCOLS), BF16),
            pltpu.VMEM((Z, BLK, KCOLS), BF16),
            pltpu.VMEM((Z, WAVES * ROWS * W, BLK), F32),
            pltpu.VMEM((Z - 1, WAVES * ROWS * W, BLK), F32),
            pltpu.VMEM((WAVES * ROWS * W, BLK), F32),
            pltpu.VMEM((XH, ROWS * W, BLK), F32),
            pltpu.VMEM((ROWS, W, BLK), F32),
            pltpu.VMEM((ROWS, W, BLK), F32),
            pltpu.VMEM((Y, W, BLK), F32),
            pltpu.VMEM((ROWS, 32, BLK), F32),
            pltpu.VMEM((32, BLK), F32),
            pltpu.VMEM((COLS, 32, BLK), F32),
            pltpu.VMEM((Y, W, BLK), F32),
            dma((Z,)),
            dma((Z,)),
            dma((Z,)),
            dma((2,)),
            dma((8,)),
            dma((8,)),
            dma((8,)),
            dma((8,)),
            dma((2,)),
            dma((4,)),
            dma((4,)),
            dma((2,)),
            dma((2,)),
            dma((8,)),
            dma((8,)),
            dma((ROWS,)),
            dma((ROWS,)),
            dma((4, Z - 1)),
            dma((4, Z - 1)),
            dma((4,)),
            dma((2, 2)),
            dma((ROWS,)),
            dma((ROWS,)),
            dma((COLS,)),
            dma((COLS,)),
            dma((ROWS,)),
            dma((ROWS,)),
        ],
        compiler_params=pltpu.CompilerParams(
            collective_id=0, has_side_effects=True, vmem_limit_bytes=60 * 1024 * 1024
        ),
        name="wave",
    )(table, lower_panel, diag_inverse, ancestor)


R_BLOCKS = 128


def solution(mesh):
    finer = Mesh(
        mesh.devices.reshape(Y, CORES, Z, XH, WAVES),
        ("row_0", "row_1", "col_0", "col_1", "wave"),
    )
    placed = (P("wave", None, COL), P("wave", None, None), P(ROW, COL_WAVE), P("wave", None))
    return jax.shard_map(
        per_device,
        mesh=finer,
        in_specs=placed,
        out_specs=(P("wave", None, ROW_COL), P("wave", None, None)),
        check_vma=False,
    )
```

```python
import jax
import jax.numpy as jnp
from jax import lax
from jax.experimental import pallas as pl
from jax.experimental.pallas import tpu as pltpu
from jax.sharding import Mesh
from jax.sharding import PartitionSpec as P

W = 64
BLK = 128
Y, CORES, Z, XH, WAVES = 4, 2, 8, 2, 2
ROWS = Y * CORES
COLS = Z * XH
KCOLS = 1024
HALF = KCOLS // 2
COL = ("col_0", "col_1")
ROW = ("row_0", "row_1")
ROW_COL = ("row_0", "row_1", "col_0", "col_1")
COL_WAVE = ("col_0", "col_1", "wave")
MESH = pl.DeviceIdType.MESH
HIGHEST = lax.Precision.HIGHEST
F32 = jnp.float32
BF16 = jnp.bfloat16


def remote(src, dst, send, recv, **device):
    return pltpu.make_async_remote_copy(
        src_ref=src,
        dst_ref=dst,
        send_sem=send,
        recv_sem=recv,
        device_id=device,
        device_id_type=MESH,
    )


def halves(value):
    high = value.astype(BF16)
    return high, (value - high.astype(F32)).astype(BF16)


def dot_last(left, right, precision=None):
    return lax.dot_general(
        left, right, (((1,), (1,)), ((), ())), precision=precision, preferred_element_type=F32
    )


def dot_first(left, right):
    return lax.dot_general(
        left, right, (((0,), (0,)), ((), ())), precision=HIGHEST, preferred_element_type=F32
    )


def kernel(
    pattern,
    lower_hbm,
    diag_hbm,
    ancestor,
    panel_out,
    block_out,
    lower,
    diag,
    packed,
    dense,
    dense_hi,
    dense_lo,
    abuf,
    a_hi,
    a_lo,
    part,
    up_in,
    down_in,
    summed,
    cross_in,
    row_blocks,
    own_rows,
    update,
    row_in,
    col_in,
    total,
    held,
    in_sem,
    a_send,
    a_recv,
    a_loc,
    h_sem,
    zp_send,
    zp_recv,
    zm_send,
    zm_recv,
    w_sem,
    y_send,
    y_recv,
    f_send,
    f_recv,
    c_send,
    c_recv,
    b_send,
    b_recv,
    up_send,
    up_recv,
    down_send,
    down_recv,
    x_send,
    x_recv,
    u_send,
    u_recv,
    v_send,
    v_recv,
    t_send,
    t_recv,
):
    y = lax.axis_index("row_0")
    k = lax.axis_index("row_1")
    z = lax.axis_index("col_0")
    h = lax.axis_index("col_1")
    w = lax.axis_index("wave")
    r = y * CORES + k
    c = z * XH + h

    def row_peer(offset):
        other = (r + offset) % ROWS
        return other, {"row_0": other // CORES, "row_1": other % CORES}

    def side_peer(offset):
        other, device = row_peer(offset // XH)
        side = (h + offset % XH) % XH
        return other, side, {**device, "col_1": side}

    barrier = pltpu.get_barrier_semaphore()

    def greet(device):
        pl.semaphore_signal(barrier, inc=1, device_id=device, device_id_type=MESH)

    take_lower = pltpu.make_async_copy(lower_hbm.at[r], lower, in_sem.at[0])
    take_diag = pltpu.make_async_copy(diag_hbm, diag, in_sem.at[1])
    take_lower.start()
    take_diag.start()
    for offset in range(1, Z):
        greet({"col_0": (z + offset) % Z})
    for offset in range(1, ROWS * XH):
        greet(side_peer(offset)[2])
    greet({"wave": 1 - w})
    greet({"col_1": 1 - h, "wave": 1 - w})

    places = [(z + offset) % Z for offset in (4, 3, 5, 2, 6, 1, 7, 0)]
    local = [
        pltpu.make_async_copy(ancestor.at[places[d], w], abuf.at[d, w], a_loc.at[d])
        for d in range(Z)
    ]
    for copy in local:
        copy.start()
    take_lower.wait()
    take_diag.wait()
    normed = dot_first(diag[r], lower[...])
    slot = 2 * c
    packed[slot] = normed[:, :BLK]
    packed[slot + 1] = normed[:, BLK:]

    own_block = r * COLS + c
    wanted = [8 * c + j for j in range(8)] + [row * COLS + c for row in range(ROWS)]

    def look(m, carry):
        block = pattern[r, m]
        found = [jnp.where(block == goal, m + 1, old) for goal, old in zip(wanted, carry[:16])]
        kept = [
            jnp.where(pattern[s, m] == own_block, 1, old) for s, old in enumerate(carry[16:])
        ]
        return tuple(found + kept)

    looked = lax.fori_loop(0, 32, look, (jnp.int32(0),) * 24)
    for s in range(ROWS):
        held[s] = looked[16 + s]

    pl.semaphore_wait(barrier, 2 + (ROWS * XH - 1) + (Z - 1))

    def pair_at(place, side):
        return packed.at[pl.ds(2 * (place * XH + side), 2)]

    trade = remote(pair_at(z, h), pair_at(z, h), h_sem.at[0], h_sem.at[1], col_1=1 - h)
    trade.start()

    a_copies = [
        remote(
            ancestor.at[places[d], 1 - w],
            abuf.at[d, w],
            a_send.at[d],
            a_recv.at[d],
            wave=1 - w,
        )
        for d in range(Z)
    ]
    z_up, z_down = (z + 1) % Z, (z + Z - 1) % Z

    def z_gather(step, own, up):
        side = h if own == 0 else 1 - h
        source = (z + Z - (step - 1)) % Z if up else (z + step - 1) % Z
        if step < 4:
            view = pair_at(source, side)
        else:
            view = packed.at[pl.ds(2 * (source * XH + side) + (0 if up else 1), 1)]
        send, recv = (zp_send, zp_recv) if up else (zm_send, zm_recv)
        slot_id = 2 * (step - 1) + own
        return remote(
            view, view, send.at[slot_id], recv.at[slot_id], col_0=z_up if up else z_down
        )

    gathers = {}
    for step in range(1, 5):
        for own in range(2):
            if step == 1 and own == 1:
                trade.wait_recv()
            for up in (True, False):
                if step > 1:
                    gathers[step - 1, own, up].wait_recv()
                copy = z_gather(step, own, up)
                copy.start()
                gathers[step, own, up] = copy
        if step <= 2:
            a_copies[step - 1].start()
    for s in range(ROWS):
        block_out[s] = dot_first(diag[s], diag[s])
    for own in range(2):
        for up in (True, False):
            gathers[4, own, up].wait_recv()

    def placed(found):
        value = packed[jnp.maximum(found - 1, 0)]
        return jnp.where(found > 0, value, jnp.zeros_like(value))

    for j in range(8):
        dense[0, :, j * BLK : (j + 1) * BLK] = placed(looked[j])

    def spot(item, dy, core):
        return (item * Y + dy) * CORES + core

    def spread(source, target, send, recv, **device):
        return remote(
            dense.at[spot(*source)], dense.at[spot(*target)], send, recv, **device
        )

    y_up, y_down = (y + 1) % Y, (y + Y - 1) % Y
    waves = (w, 1 - w)

    def y_copy(item, up):
        slot_id = 2 * item + (0 if up else 1)
        return spread(
            (item, 0, 0),
            (item, 3 if up else 1, 0),
            y_send.at[slot_id],
            y_recv.at[slot_id],
            row_0=y_up if up else y_down,
        )

    def core_copy(item, dy):
        slot_id = 4 * item + dy
        return spread(
            (item, dy, 0), (item, dy, 1), c_send.at[slot_id], c_recv.at[slot_id], row_1=1 - k
        )

    wave_copy = spread((0, 0, 0), (1, 0, 0), w_sem.at[0], w_sem.at[1], wave=1 - w)
    y_copies = {(item, up): y_copy(item, up) for item in range(2) for up in (True, False)}
    core_copies = {(item, dy): core_copy(item, dy) for item in range(2) for dy in range(Y)}
    far_up = spread((0, 3, 0), (0, 2, 0), f_send.at[0], f_recv.at[0], row_0=y_up)
    far_down = spread((1, 1, 0), (1, 2, 0), f_send.at[1], f_recv.at[1], row_0=y_down)

    units = ((0, 0), (0, 1), (0, 3), (1, 0), (0, 2), (1, 1), (1, 3), (1, 2))

    def split_unit(unit):
        item, dy = units[unit]
        core_copies[item, dy].wait_recv()
        for core in range(CORES):
            rows = slice(unit * BLK + core * W, unit * BLK + (core + 1) * W)
            high, low = halves(dense[spot(item, dy, core)])
            dense_hi[rows, :] = high
            dense_lo[rows, :] = low

    def split_ancestor(d):
        local[d].wait()
        a_copies[d].wait_recv()
        for side in range(WAVES):
            high, low = halves(abuf[d, side])
            a_hi[d, :, side * HALF : (side + 1) * HALF] = high
            a_lo[d, :, side * HALF : (side + 1) * HALF] = low

    def multiply(group, first, count):
        right_hi = a_hi[first : first + count].reshape(count * BLK, KCOLS)
        right_lo = a_lo[first : first + count].reshape(count * BLK, KCOLS)
        for start in range(group * 512, group * 512 + 512, 256):
            rows = slice(start, start + 256)
            left_hi, left_lo = dense_hi[rows, :], dense_lo[rows, :]
            product = (
                dot_last(left_hi, right_lo) + dot_last(left_lo, right_hi)
            ) + dot_last(left_hi, right_hi)
            for d in range(count):
                part[first + d, rows, :] = product[:, d * BLK : (d + 1) * BLK]

    def rows_of(unit):
        return pl.ds(unit * BLK, BLK)

    def chain(t, unit, up):
        slot_id = 0 if t == 0 else (2 * t - 1 if up else 2 * t)
        send, recv, into = (up_send, up_recv, up_in) if up else (down_send, down_recv, down_in)
        return remote(
            part.at[slot_id, rows_of(unit)],
            into.at[t, rows_of(unit)],
            send.at[t, unit],
            recv.at[t, unit],
            col_0=z_up if up else z_down,
        )

    chains = []

    def send_on(t, unit, up):
        copy = chain(t, unit, up)
        copy.start()
        chains.append(copy)

    def first_step(group):
        for unit in range(4 * group, 4 * group + 4):
            send_on(0, unit, unit % 2 == 0)

    def next_step(group, t):
        for unit in range(4 * group, 4 * group + 4):
            for up in (True, False):
                if t > 1 or (unit % 2 == 0) == up:
                    chain(t - 1, unit, up).wait_recv()
                    slot_id = 2 * t - 1 if up else 2 * t
                    into = up_in if up else down_in
                    part[slot_id, rows_of(unit), :] = (
                        part[slot_id, rows_of(unit), :] + into[t - 1, rows_of(unit), :]
                    )
                send_on(t, unit, up)

    def cross_copy(unit):
        item, dy = units[unit]
        return remote(
            summed.at[rows_of(unit)],
            cross_in.at[h, dy],
            x_send.at[unit],
            x_recv.at[h, dy],
            col_1=w,
            wave=waves[item],
        )

    def last_step(group):
        for unit in range(4 * group, 4 * group + 4):
            item, dy = units[unit]
            chain(3, unit, True).wait_recv()
            chain(3, unit, False).wait_recv()
            summed[rows_of(unit), :] = (
                part[7, rows_of(unit), :] + up_in[3, rows_of(unit), :]
            ) + down_in[3, rows_of(unit), :]
            if item == 1:
                cross_copy(unit).start()
            else:

                @pl.when(h != w)
                def _():
                    cross_copy(unit).start()

                @pl.when(h == w)
                def _():
                    cross_in[h, dy] = summed[rows_of(unit), :]

    wave_copy.start()
    y_copies[0, True].start()
    y_copies[0, False].start()
    core_copies[0, 0].start()
    for d in range(2, Z):
        a_copies[d].start()
    for row in range(ROWS):
        row_blocks[row] = placed(looked[8 + row])
    own_rows[r] = row_blocks[r]
    split_ancestor(0)
    split_unit(0)
    y_copies[0, True].wait_recv()
    far_up.start()
    core_copies[0, 3].start()
    y_copies[0, False].wait_recv()
    core_copies[0, 1].start()
    wave_copy.wait_recv()
    y_copies[1, True].start()
    y_copies[1, False].start()
    core_copies[1, 0].start()
    split_unit(1)
    split_unit(2)
    split_unit(3)
    multiply(0, 0, 1)
    first_step(0)
    split_ancestor(1)
    split_ancestor(2)
    multiply(0, 1, 2)
    y_copies[1, False].wait_recv()
    far_down.start()
    core_copies[1, 1].start()
    y_copies[1, True].wait_recv()
    core_copies[1, 3].start()
    block_copies = []
    for offset in range(1, ROWS):
        other, device = row_peer(offset)
        copy = remote(
            row_blocks.at[other],
            own_rows.at[r],
            b_send.at[offset],
            b_recv.at[offset],
            **device,
        )
        copy.start()
        block_copies.append(copy)
    next_step(0, 1)
    far_up.wait_recv()
    core_copies[0, 2].start()
    split_ancestor(3)
    split_ancestor(4)
    multiply(0, 3, 2)
    split_unit(4)
    split_unit(5)
    split_unit(6)
    next_step(0, 2)
    far_down.wait_recv()
    core_copies[1, 2].start()
    split_unit(7)
    multiply(1, 0, 1)
    first_step(1)
    multiply(1, 1, 2)
    split_ancestor(5)
    split_ancestor(6)
    multiply(0, 5, 2)
    next_step(0, 3)
    next_step(1, 1)
    multiply(1, 3, 2)
    next_step(1, 2)
    multiply(1, 5, 2)
    split_ancestor(7)
    multiply(0, 7, 1)
    last_step(0)
    next_step(1, 3)
    multiply(1, 7, 1)
    last_step(1)

    for copy in block_copies:
        copy.wait_recv()

    for dy in (0, 1, 3, 2):
        for side in range(XH):

            @pl.when(jnp.logical_not(jnp.logical_and(h == w, h == side)))
            def _():
                remote(
                    summed.at[rows_of(0)],
                    cross_in.at[side, dy],
                    x_send.at[0],
                    x_recv.at[side, dy],
                    col_1=1 - h,
                ).wait_recv()

        squares = []
        for core in range(CORES):
            s = ((y + dy) % Y) * CORES + (k if core == 0 else 1 - k)
            rows = slice(core * W, (core + 1) * W)
            value = -(cross_in[0, dy, rows, :] + cross_in[1, dy, rows, :])
            value = jnp.where(held[s] > 0, value, jnp.zeros_like(value))
            panel_out[s] = value
            squares.append(dot_last(own_rows[s], value, HIGHEST))
        first = jnp.where(k == 0, squares[0], squares[1])
        update[(y + dy) % Y, :, :W] = first
        update[(y + dy) % Y, :, W:] = jnp.where(k == 0, squares[1], squares[0])

    def share(row, side):
        start = (row % CORES) * 32 + side * 16
        return pl.ds(pl.multiple_of(start, 16), 16)

    u_copies = []
    for offset in range(1, ROWS * XH):
        other, side, device = side_peer(offset)
        copy = remote(
            update.at[other // CORES, share(other, side)],
            row_in.at[offset],
            u_send.at[offset],
            u_recv.at[offset],
            **device,
        )
        copy.start()
        u_copies.append(copy)
    mine = share(r, h)
    partial = update[y, mine, :]
    for offset in range(1, ROWS * XH):
        u_copies[offset - 1].wait_recv()
        partial = partial + row_in[offset]
    col_in[0] = partial
    v_copies = []
    for offset in (4, 3, 5, 2, 6, 1, 7):
        copy = remote(
            col_in.at[0],
            col_in.at[offset],
            v_send.at[offset],
            v_recv.at[offset],
            col_0=(z + offset) % Z,
        )
        copy.start()
        v_copies.append(copy)
    for copy in v_copies:
        copy.wait_recv()
    whole = col_in[z]
    for owner in range(1, Z):
        whole = whole + col_in[(z + Z - owner) % Z]
    total[y, mine, :] = whole
    t_copies = []
    for offset in range(1, ROWS * XH):
        copy = remote(
            total.at[y, mine],
            total.at[y, mine],
            t_send.at[offset],
            t_recv.at[offset],
            **side_peer(offset)[2],
        )
        copy.start()
        t_copies.append(copy)
    for copy in t_copies:
        copy.wait_recv()
    for s in range(ROWS):
        lanes = slice((s % 2) * W, (s % 2 + 1) * W)
        block_out[s] = block_out[s] - total[s // 2, :, lanes]

    trade.wait_send()
    for copy in gathers.values():
        copy.wait_send()
    for copy in a_copies:
        copy.wait_send()
    wave_copy.wait_send()
    for copy in y_copies.values():
        copy.wait_send()
    for copy in core_copies.values():
        copy.wait_send()
    far_up.wait_send()
    far_down.wait_send()
    for copy in chains + block_copies + u_copies + v_copies + t_copies:
        copy.wait_send()
    for unit in range(8):
        if units[unit][0] == 1:
            cross_copy(unit).wait_send()
        else:

            @pl.when(h != w)
            def _():
                cross_copy(unit).wait_send()


def finish(panel_in, block_in, panel_out, block_out):
    panel_out[...] = panel_in[...]
    block_out[...] = block_in[...]


def per_device(lower_panel, diag_inverse, ancestor_inverse, pattern):
    ancestor = ancestor_inverse.reshape(Z, XH, BLK, HALF)
    vmem = pl.BlockSpec(memory_space=pltpu.VMEM)
    hbm = pl.BlockSpec(memory_space=pl.ANY)
    dma = pltpu.SemaphoreType.DMA
    sibs = WAVES * ROWS * W
    outs = (
        jax.ShapeDtypeStruct((ROWS, W, BLK), F32),
        jax.ShapeDtypeStruct((ROWS, W, W), F32),
    )
    panel, block = pl.pallas_call(
        kernel,
        out_shape=outs,
        in_specs=[pl.BlockSpec(memory_space=pltpu.SMEM), hbm, hbm, hbm],
        out_specs=(vmem, vmem),
        scratch_shapes=[
            pltpu.VMEM((W, 2 * BLK), F32),
            pltpu.VMEM((ROWS, W, W), F32),
            pltpu.VMEM((32, W, BLK), F32),
            pltpu.VMEM((WAVES * ROWS, W, KCOLS), F32),
            pltpu.VMEM((sibs, KCOLS), BF16),
            pltpu.VMEM((sibs, KCOLS), BF16),
            pltpu.VMEM((Z, WAVES, BLK, HALF), F32),
            pltpu.VMEM((Z, BLK, KCOLS), BF16),
            pltpu.VMEM((Z, BLK, KCOLS), BF16),
            pltpu.VMEM((Z, sibs, BLK), F32),
            pltpu.VMEM((4, sibs, BLK), F32),
            pltpu.VMEM((4, sibs, BLK), F32),
            pltpu.VMEM((sibs, BLK), F32),
            pltpu.VMEM((XH, Y, 2 * W, BLK), F32),
            pltpu.VMEM((ROWS, W, BLK), F32),
            pltpu.VMEM((ROWS, W, BLK), F32),
            pltpu.VMEM((Y, W, BLK), F32),
            pltpu.VMEM((ROWS * XH, 16, BLK), F32),
            pltpu.VMEM((Z, 16, BLK), F32),
            pltpu.VMEM((Y, W, BLK), F32),
            pltpu.SMEM((ROWS,), jnp.int32),
            dma((2,)),
            dma((Z,)),
            dma((Z,)),
            dma((Z,)),
            dma((2,)),
            dma((8,)),
            dma((8,)),
            dma((8,)),
            dma((8,)),
            dma((2,)),
            dma((4,)),
            dma((4,)),
            dma((2,)),
            dma((2,)),
            dma((8,)),
            dma((8,)),
            dma((ROWS,)),
            dma((ROWS,)),
            dma((4, 8)),
            dma((4, 8)),
            dma((4, 8)),
            dma((4, 8)),
            dma((8,)),
            dma((2, 4)),
            dma((ROWS * XH,)),
            dma((ROWS * XH,)),
            dma((Z,)),
            dma((Z,)),
            dma((ROWS * XH,)),
            dma((ROWS * XH,)),
        ],
        compiler_params=pltpu.CompilerParams(
            collective_id=0, has_side_effects=True, vmem_limit_bytes=60 * 1024 * 1024
        ),
        name="wave",
    )(pattern, lower_panel, diag_inverse, ancestor)
    return pl.pallas_call(
        finish,
        out_shape=outs,
        in_specs=[vmem, vmem],
        out_specs=(vmem, vmem),
        name="finish",
    )(panel, block)


def solution(mesh):
    finer = Mesh(
        mesh.devices.reshape(Y, CORES, Z, XH, WAVES),
        ("row_0", "row_1", "col_0", "col_1", "wave"),
    )
    placed = (P("wave", None, COL), P("wave", None, None), P(ROW, COL_WAVE), P("wave", None))
    return jax.shard_map(
        per_device,
        mesh=finer,
        in_specs=placed,
        out_specs=(P("wave", None, ROW_COL), P("wave", None, None)),
        check_vma=False,
    )
```

```python
import jax
import jax.numpy as jnp
from jax import lax
from jax.experimental import pallas as pl
from jax.experimental.pallas import tpu as pltpu
from jax.sharding import Mesh
from jax.sharding import PartitionSpec as P

W = 64
BLK = 128
Y, CORES, Z, XH, WAVES = 4, 2, 8, 2, 2
ROWS = Y * CORES
COLS = Z * XH
KCOLS = 1024
HALF = KCOLS // 2
COL = ("col_0", "col_1")
ROW = ("row_0", "row_1")
ROW_COL = ("row_0", "row_1", "col_0", "col_1")
COL_WAVE = ("col_0", "col_1", "wave")
MESH = pl.DeviceIdType.MESH
HIGHEST = lax.Precision.HIGHEST
F32 = jnp.float32
BF16 = jnp.bfloat16


def remote(src, dst, send, recv, **device):
    return pltpu.make_async_remote_copy(
        src_ref=src,
        dst_ref=dst,
        send_sem=send,
        recv_sem=recv,
        device_id=device,
        device_id_type=MESH,
    )


def halves(value):
    high = value.astype(BF16)
    return high, (value - high.astype(F32)).astype(BF16)


def dot_last(left, right, precision=None):
    return lax.dot_general(
        left, right, (((1,), (1,)), ((), ())), precision=precision, preferred_element_type=F32
    )


def dot_first(left, right):
    return lax.dot_general(
        left, right, (((0,), (0,)), ((), ())), precision=HIGHEST, preferred_element_type=F32
    )


def kernel(
    pattern,
    lower_hbm,
    diag_hbm,
    ancestor,
    panel_out,
    block_out,
    lower,
    diag,
    packed,
    dense,
    dense_hi,
    dense_lo,
    abuf,
    a_hi,
    a_lo,
    part,
    up_in,
    down_in,
    summed,
    cross_in,
    row_blocks,
    own_rows,
    update,
    row_in,
    col_in,
    total,
    held,
    in_sem,
    a_send,
    a_recv,
    a_loc,
    h_sem,
    zp_send,
    zp_recv,
    zm_send,
    zm_recv,
    w_sem,
    y_send,
    y_recv,
    f_send,
    f_recv,
    c_send,
    c_recv,
    b_send,
    b_recv,
    up_send,
    up_recv,
    down_send,
    down_recv,
    x_send,
    x_recv,
    u_send,
    u_recv,
    v_send,
    v_recv,
    t_send,
    t_recv,
):
    y = lax.axis_index("row_0")
    k = lax.axis_index("row_1")
    z = lax.axis_index("col_0")
    h = lax.axis_index("col_1")
    w = lax.axis_index("wave")
    r = y * CORES + k
    c = z * XH + h

    def row_peer(offset):
        other = (r + offset) % ROWS
        return other, {"row_0": other // CORES, "row_1": other % CORES}

    def side_peer(offset):
        other, device = row_peer(offset // XH)
        side = (h + offset % XH) % XH
        return other, side, {**device, "col_1": side}

    barrier = pltpu.get_barrier_semaphore()

    def greet(device):
        pl.semaphore_signal(barrier, inc=1, device_id=device, device_id_type=MESH)

    take_lower = pltpu.make_async_copy(lower_hbm.at[r], lower, in_sem.at[0])
    take_diag = pltpu.make_async_copy(diag_hbm, diag, in_sem.at[1])
    for offset in range(1, Z):
        greet({"col_0": (z + offset) % Z})
    for offset in range(1, ROWS * XH):
        greet(side_peer(offset)[2])
    greet({"wave": 1 - w})
    greet({"col_1": 1 - h, "wave": 1 - w})

    take_lower.start()
    take_diag.start()
    places = [(z + offset) % Z for offset in (4, 3, 5, 2, 6, 1, 7, 0)]
    local = [
        pltpu.make_async_copy(ancestor.at[places[d], w], abuf.at[d, w], a_loc.at[d])
        for d in range(Z)
    ]
    for copy in local:
        copy.start()
    take_lower.wait()
    take_diag.wait()
    normed = dot_first(diag[r], lower[...])
    slot = 2 * c
    packed[slot] = normed[:, :BLK]
    packed[slot + 1] = normed[:, BLK:]

    pl.semaphore_wait(barrier, 2 + (ROWS * XH - 1) + (Z - 1))

    def pair_at(place, side):
        return packed.at[pl.ds(2 * (place * XH + side), 2)]

    trade = remote(pair_at(z, h), pair_at(z, h), h_sem.at[0], h_sem.at[1], col_1=1 - h)
    trade.start()

    a_copies = [
        remote(
            ancestor.at[places[d], 1 - w],
            abuf.at[d, w],
            a_send.at[d],
            a_recv.at[d],
            wave=1 - w,
        )
        for d in range(Z)
    ]
    z_up, z_down = (z + 1) % Z, (z + Z - 1) % Z

    def z_gather(step, own, up):
        side = h if own == 0 else 1 - h
        source = (z + Z - (step - 1)) % Z if up else (z + step - 1) % Z
        if step < 4:
            view = pair_at(source, side)
        else:
            view = packed.at[pl.ds(2 * (source * XH + side) + (0 if up else 1), 1)]
        send, recv = (zp_send, zp_recv) if up else (zm_send, zm_recv)
        slot_id = 2 * (step - 1) + own
        return remote(
            view, view, send.at[slot_id], recv.at[slot_id], col_0=z_up if up else z_down
        )

    own_block = r * COLS + c
    wanted = [8 * c + j for j in range(8)] + [row * COLS + c for row in range(ROWS)]

    def look(m, carry):
        block = pattern[r, m]
        found = [jnp.where(block == goal, m + 1, old) for goal, old in zip(wanted, carry[:16])]
        kept = [
            jnp.where(pattern[s, m] == own_block, 1, old) for s, old in enumerate(carry[16:])
        ]
        return tuple(found + kept)

    def look_up():
        looked = lax.fori_loop(0, 32, look, (jnp.int32(0),) * 24)
        for s in range(ROWS):
            held[s] = looked[16 + s]
        return looked

    gathers = {}
    for step in range(1, 5):
        for own in range(2):
            if step == 1 and own == 1:
                trade.wait_recv()
            for up in (True, False):
                if step > 1:
                    gathers[step - 1, own, up].wait_recv()
                copy = z_gather(step, own, up)
                copy.start()
                gathers[step, own, up] = copy
        if step <= 3:
            a_copies[step - 1].start()
        if step == 1:
            looked = look_up()
        if step == 2:
            for s in range(ROWS):
                block_out[s] = dot_first(diag[s], diag[s])
    for own in range(2):
        for up in (True, False):
            gathers[4, own, up].wait_recv()

    def placed(found):
        value = packed[jnp.maximum(found - 1, 0)]
        return jnp.where(found > 0, value, jnp.zeros_like(value))

    for j in range(8):
        dense[0, :, j * BLK : (j + 1) * BLK] = placed(looked[j])

    def spot(item, dy, core):
        return (item * Y + dy) * CORES + core

    def spread(source, target, send, recv, **device):
        return remote(
            dense.at[spot(*source)], dense.at[spot(*target)], send, recv, **device
        )

    y_up, y_down = (y + 1) % Y, (y + Y - 1) % Y
    waves = (w, 1 - w)

    def y_copy(item, up):
        slot_id = 2 * item + (0 if up else 1)
        return spread(
            (item, 0, 0),
            (item, 3 if up else 1, 0),
            y_send.at[slot_id],
            y_recv.at[slot_id],
            row_0=y_up if up else y_down,
        )

    def core_copy(item, dy):
        slot_id = 4 * item + dy
        return spread(
            (item, dy, 0), (item, dy, 1), c_send.at[slot_id], c_recv.at[slot_id], row_1=1 - k
        )

    wave_copy = spread((0, 0, 0), (1, 0, 0), w_sem.at[0], w_sem.at[1], wave=1 - w)
    y_copies = {(item, up): y_copy(item, up) for item in range(2) for up in (True, False)}
    core_copies = {(item, dy): core_copy(item, dy) for item in range(2) for dy in range(Y)}

    def far_copy(item, up):
        source = dense.at[spot(item, 3 if up else 1, 0), pl.ds(0 if up else W // 2, W // 2)]
        target = dense.at[spot(item, 2, 0), pl.ds(0 if up else W // 2, W // 2)]
        slot_id = 2 * item + (0 if up else 1)
        return remote(
            source,
            target,
            f_send.at[slot_id],
            f_recv.at[slot_id],
            row_0=y_up if up else y_down,
        )

    far_copies = {(item, up): far_copy(item, up) for item in range(2) for up in (True, False)}

    units = ((0, 0), (0, 1), (0, 3), (1, 0), (0, 2), (1, 1), (1, 3), (1, 2))
    groups = (range(0, 3), range(3, 5), range(5, 8))

    def split_unit(unit):
        item, dy = units[unit]
        core_copies[item, dy].wait_recv()
        for core in range(CORES):
            rows = slice(unit * BLK + core * W, unit * BLK + (core + 1) * W)
            high, low = halves(dense[spot(item, dy, core)])
            dense_hi[rows, :] = high
            dense_lo[rows, :] = low

    def split_ancestor(d):
        local[d].wait()
        a_copies[d].wait_recv()
        for side in range(WAVES):
            high, low = halves(abuf[d, side])
            a_hi[d, :, side * HALF : (side + 1) * HALF] = high
            a_lo[d, :, side * HALF : (side + 1) * HALF] = low

    def multiply(group, first, count):
        right_hi = a_hi[first : first + count].reshape(count * BLK, KCOLS)
        right_lo = a_lo[first : first + count].reshape(count * BLK, KCOLS)
        rows = slice(groups[group][0] * BLK, (groups[group][-1] + 1) * BLK)
        left_hi, left_lo = dense_hi[rows, :], dense_lo[rows, :]
        product = (
            dot_last(left_hi, right_lo) + dot_last(left_lo, right_hi)
        ) + dot_last(left_hi, right_hi)
        for d in range(count):
            part[first + d, rows, :] = product[:, d * BLK : (d + 1) * BLK]

    def rows_of(unit):
        return pl.ds(unit * BLK, BLK)

    def chain(t, unit, up):
        slot_id = 0 if t == 0 else (2 * t - 1 if up else 2 * t)
        send, recv, into = (up_send, up_recv, up_in) if up else (down_send, down_recv, down_in)
        return remote(
            part.at[slot_id, rows_of(unit)],
            into.at[t, rows_of(unit)],
            send.at[t, unit],
            recv.at[t, unit],
            col_0=z_up if up else z_down,
        )

    chains = []

    def send_on(t, unit, up):
        copy = chain(t, unit, up)
        copy.start()
        chains.append(copy)

    def first_step(group):
        for unit in groups[group]:
            send_on(0, unit, unit % 2 == 0)

    def next_step(group, t):
        for unit in groups[group]:
            for up in (True, False):
                if t > 1 or (unit % 2 == 0) == up:
                    chain(t - 1, unit, up).wait_recv()
                    slot_id = 2 * t - 1 if up else 2 * t
                    into = up_in if up else down_in
                    part[slot_id, rows_of(unit), :] = (
                        part[slot_id, rows_of(unit), :] + into[t - 1, rows_of(unit), :]
                    )
                send_on(t, unit, up)

    def cross_copy(unit):
        item, dy = units[unit]
        return remote(
            summed.at[rows_of(unit)],
            cross_in.at[h, dy],
            x_send.at[unit],
            x_recv.at[h, dy],
            col_1=w,
            wave=waves[item],
        )

    def last_step(group):
        for unit in groups[group]:
            item, dy = units[unit]
            chain(3, unit, True).wait_recv()
            chain(3, unit, False).wait_recv()
            summed[rows_of(unit), :] = (
                part[7, rows_of(unit), :] + up_in[3, rows_of(unit), :]
            ) + down_in[3, rows_of(unit), :]
            if item == 1:
                cross_copy(unit).start()
            else:

                @pl.when(h != w)
                def _():
                    cross_copy(unit).start()

                @pl.when(h == w)
                def _():
                    cross_in[h, dy] = summed[rows_of(unit), :]

    wave_copy.start()
    y_copies[0, True].start()
    y_copies[0, False].start()
    core_copies[0, 0].start()
    for d in range(3, Z):
        a_copies[d].start()
    for row in range(ROWS):
        row_blocks[row] = placed(looked[8 + row])
    own_rows[r] = row_blocks[r]
    split_ancestor(0)
    split_ancestor(1)
    split_unit(0)
    y_copies[0, True].wait_recv()
    far_copies[0, True].start()
    core_copies[0, 3].start()
    y_copies[0, False].wait_recv()
    far_copies[0, False].start()
    core_copies[0, 1].start()
    split_unit(1)
    split_unit(2)
    multiply(0, 0, 1)
    first_step(0)
    wave_copy.wait_recv()
    y_copies[1, True].start()
    y_copies[1, False].start()
    core_copies[1, 0].start()
    split_ancestor(2)
    multiply(0, 1, 2)
    for up in (True, False):
        far_copies[0, up].wait_recv()
    core_copies[0, 2].start()
    next_step(0, 1)
    split_unit(3)
    split_unit(4)
    multiply(1, 0, 1)
    first_step(1)
    multiply(1, 1, 2)
    y_copies[1, True].wait_recv()
    far_copies[1, True].start()
    core_copies[1, 3].start()
    y_copies[1, False].wait_recv()
    far_copies[1, False].start()
    core_copies[1, 1].start()
    block_copies = []
    for offset in range(1, ROWS):
        other, device = row_peer(offset)
        copy = remote(
            row_blocks.at[other],
            own_rows.at[r],
            b_send.at[offset],
            b_recv.at[offset],
            **device,
        )
        copy.start()
        block_copies.append(copy)
    next_step(1, 1)
    split_ancestor(3)
    split_ancestor(4)
    multiply(0, 3, 2)
    next_step(0, 2)
    multiply(1, 3, 2)
    split_unit(5)
    split_unit(6)
    next_step(1, 2)
    for up in (True, False):
        far_copies[1, up].wait_recv()
    core_copies[1, 2].start()
    split_unit(7)
    multiply(2, 0, 1)
    first_step(2)
    multiply(2, 1, 2)
    next_step(2, 1)
    split_ancestor(5)
    split_ancestor(6)
    multiply(0, 5, 2)
    next_step(0, 3)
    multiply(1, 5, 2)
    next_step(1, 3)
    multiply(2, 3, 2)
    next_step(2, 2)
    multiply(2, 5, 2)
    split_ancestor(7)
    multiply(0, 7, 1)
    multiply(1, 7, 1)
    last_step(0)
    multiply(2, 7, 1)
    last_step(1)
    next_step(2, 3)
    last_step(2)

    for copy in block_copies:
        copy.wait_recv()

    for dy in (0, 1, 3, 2):
        for side in range(XH):

            @pl.when(jnp.logical_not(jnp.logical_and(h == w, h == side)))
            def _():
                remote(
                    summed.at[rows_of(0)],
                    cross_in.at[side, dy],
                    x_send.at[0],
                    x_recv.at[side, dy],
                    col_1=1 - h,
                ).wait_recv()

        squares = []
        for core in range(CORES):
            s = ((y + dy) % Y) * CORES + (k if core == 0 else 1 - k)
            rows = slice(core * W, (core + 1) * W)
            value = -(cross_in[0, dy, rows, :] + cross_in[1, dy, rows, :])
            value = jnp.where(held[s] > 0, value, jnp.zeros_like(value))
            panel_out[s] = value
            squares.append(dot_last(own_rows[s], value, HIGHEST))
        first = jnp.where(k == 0, squares[0], squares[1])
        update[(y + dy) % Y, :, :W] = first
        update[(y + dy) % Y, :, W:] = jnp.where(k == 0, squares[1], squares[0])

    def share(row, side):
        start = (row % CORES) * 32 + side * 16
        return pl.ds(pl.multiple_of(start, 16), 16)

    u_copies = []
    for offset in range(1, ROWS * XH):
        other, side, device = side_peer(offset)
        copy = remote(
            update.at[other // CORES, share(other, side)],
            row_in.at[offset],
            u_send.at[offset],
            u_recv.at[offset],
            **device,
        )
        copy.start()
        u_copies.append(copy)
    mine = share(r, h)
    partial = update[y, mine, :]
    for offset in range(1, ROWS * XH):
        u_copies[offset - 1].wait_recv()
        partial = partial + row_in[offset]
    col_in[0] = partial
    v_copies = []
    for offset in (4, 3, 5, 2, 6, 1, 7):
        copy = remote(
            col_in.at[0],
            col_in.at[offset],
            v_send.at[offset],
            v_recv.at[offset],
            col_0=(z + offset) % Z,
        )
        copy.start()
        v_copies.append(copy)
    for copy in v_copies:
        copy.wait_recv()
    whole = col_in[z]
    for owner in range(1, Z):
        whole = whole + col_in[(z + Z - owner) % Z]
    total[y, mine, :] = whole
    t_copies = []
    for offset in range(1, ROWS * XH):
        copy = remote(
            total.at[y, mine],
            total.at[y, mine],
            t_send.at[offset],
            t_recv.at[offset],
            **side_peer(offset)[2],
        )
        copy.start()
        t_copies.append(copy)
    for copy in t_copies:
        copy.wait_recv()
    for s in range(ROWS):
        lanes = slice((s % 2) * W, (s % 2 + 1) * W)
        block_out[s] = block_out[s] - total[s // 2, :, lanes]

    trade.wait_send()
    for copy in gathers.values():
        copy.wait_send()
    for copy in a_copies:
        copy.wait_send()
    wave_copy.wait_send()
    for copy in y_copies.values():
        copy.wait_send()
    for copy in core_copies.values():
        copy.wait_send()
    for copy in far_copies.values():
        copy.wait_send()
    for copy in chains + block_copies + u_copies + v_copies + t_copies:
        copy.wait_send()
    for unit in range(8):
        if units[unit][0] == 1:
            cross_copy(unit).wait_send()
        else:

            @pl.when(h != w)
            def _():
                cross_copy(unit).wait_send()


def per_device(lower_panel, diag_inverse, ancestor_inverse, pattern):
    ancestor = ancestor_inverse.reshape(Z, XH, BLK, HALF)
    vmem = pl.BlockSpec(memory_space=pltpu.VMEM)
    hbm = pl.BlockSpec(memory_space=pl.ANY)
    dma = pltpu.SemaphoreType.DMA
    sibs = WAVES * ROWS * W
    outs = (
        jax.ShapeDtypeStruct((ROWS, W, BLK), F32),
        jax.ShapeDtypeStruct((ROWS, W, W), F32),
    )
    return pl.pallas_call(
        kernel,
        out_shape=tuple(pltpu.VMEM(out.shape, out.dtype) for out in outs),
        in_specs=[pl.BlockSpec(memory_space=pltpu.SMEM), hbm, hbm, hbm],
        out_specs=(vmem, vmem),
        scratch_shapes=[
            pltpu.VMEM((W, 2 * BLK), F32),
            pltpu.VMEM((ROWS, W, W), F32),
            pltpu.VMEM((32, W, BLK), F32),
            pltpu.VMEM((WAVES * ROWS, W, KCOLS), F32),
            pltpu.VMEM((sibs, KCOLS), BF16),
            pltpu.VMEM((sibs, KCOLS), BF16),
            pltpu.VMEM((Z, WAVES, BLK, HALF), F32),
            pltpu.VMEM((Z, BLK, KCOLS), BF16),
            pltpu.VMEM((Z, BLK, KCOLS), BF16),
            pltpu.VMEM((Z, sibs, BLK), F32),
            pltpu.VMEM((4, sibs, BLK), F32),
            pltpu.VMEM((4, sibs, BLK), F32),
            pltpu.VMEM((sibs, BLK), F32),
            pltpu.VMEM((XH, Y, 2 * W, BLK), F32),
            pltpu.VMEM((ROWS, W, BLK), F32),
            pltpu.VMEM((ROWS, W, BLK), F32),
            pltpu.VMEM((Y, W, BLK), F32),
            pltpu.VMEM((ROWS * XH, 16, BLK), F32),
            pltpu.VMEM((Z, 16, BLK), F32),
            pltpu.VMEM((Y, W, BLK), F32),
            pltpu.SMEM((ROWS,), jnp.int32),
            dma((2,)),
            dma((Z,)),
            dma((Z,)),
            dma((Z,)),
            dma((2,)),
            dma((8,)),
            dma((8,)),
            dma((8,)),
            dma((8,)),
            dma((2,)),
            dma((4,)),
            dma((4,)),
            dma((4,)),
            dma((4,)),
            dma((8,)),
            dma((8,)),
            dma((ROWS,)),
            dma((ROWS,)),
            dma((4, 8)),
            dma((4, 8)),
            dma((4, 8)),
            dma((4, 8)),
            dma((8,)),
            dma((2, 4)),
            dma((ROWS * XH,)),
            dma((ROWS * XH,)),
            dma((Z,)),
            dma((Z,)),
            dma((ROWS * XH,)),
            dma((ROWS * XH,)),
        ],
        compiler_params=pltpu.CompilerParams(
            collective_id=0, has_side_effects=True, vmem_limit_bytes=60 * 1024 * 1024
        ),
        name="wave",
    )(pattern, lower_panel, diag_inverse, ancestor)


def solution(mesh):
    finer = Mesh(
        mesh.devices.reshape(Y, CORES, Z, XH, WAVES),
        ("row_0", "row_1", "col_0", "col_1", "wave"),
    )
    placed = (P("wave", None, COL), P("wave", None, None), P(ROW, COL_WAVE), P("wave", None))
    return jax.shard_map(
        per_device,
        mesh=finer,
        in_specs=placed,
        out_specs=(P("wave", None, ROW_COL), P("wave", None, None)),
        check_vma=False,
    )
```

```python
import jax
import jax.numpy as jnp
from jax import lax
from jax.experimental import pallas as pl
from jax.experimental.pallas import tpu as pltpu
from jax.sharding import Mesh
from jax.sharding import PartitionSpec as P

W = 64
BLK = 128
PART = 32
Y, CORES, Z, XH, WAVES = 4, 2, 8, 2, 2
ROWS = Y * CORES
COLS = Z * XH
KCOLS = 1024
HALF = KCOLS // 2
COL = ("col_0", "col_1")
ROW = ("row_0", "row_1")
ROW_COL = ("row_0", "row_1", "col_0", "col_1")
COL_WAVE = ("col_0", "col_1", "wave")
MESH = pl.DeviceIdType.MESH
HIGHEST = lax.Precision.HIGHEST
F32 = jnp.float32
BF16 = jnp.bfloat16


def remote(src, dst, send, recv, **device):
    return pltpu.make_async_remote_copy(
        src_ref=src,
        dst_ref=dst,
        send_sem=send,
        recv_sem=recv,
        device_id=device,
        device_id_type=MESH,
    )


def halves(value):
    high = value.astype(BF16)
    return high, (value - high.astype(F32)).astype(BF16)


def dot_last(left, right, precision=None):
    return lax.dot_general(
        left, right, (((1,), (1,)), ((), ())), precision=precision, preferred_element_type=F32
    )


def dot_first(left, right):
    return lax.dot_general(
        left, right, (((0,), (0,)), ((), ())), precision=HIGHEST, preferred_element_type=F32
    )


def kernel(
    pattern,
    lower_hbm,
    diag_hbm,
    ancestor,
    panel_out,
    block_out,
    lower,
    diag,
    packed_a,
    packed_b,
    dense_a,
    dense_b,
    dense_hi,
    dense_lo,
    abuf,
    a_hi,
    a_lo,
    part,
    up_in,
    down_in,
    summed,
    cross_in,
    row_blocks,
    own_rows,
    update,
    row_in,
    col_in,
    total,
    held,
    in_sem,
    a_send,
    a_recv,
    a_loc,
    h_sem,
    zp_send,
    zp_recv,
    zm_send,
    zm_recv,
    w_sem,
    y_send,
    y_recv,
    f_send,
    f_recv,
    c_send,
    c_recv,
    b_send,
    b_recv,
    up_send,
    up_recv,
    down_send,
    down_recv,
    x_send,
    x_recv,
    u_send,
    u_recv,
    v_send,
    v_recv,
    t_send,
    t_recv,
):
    y = lax.axis_index("row_0")
    k = lax.axis_index("row_1")
    z = lax.axis_index("col_0")
    h = lax.axis_index("col_1")
    w = lax.axis_index("wave")
    r = y * CORES + k
    c = z * XH + h
    packed, dense = (packed_a, packed_b), (dense_a, dense_b)

    def row_peer(offset):
        other = (r + offset) % ROWS
        return other, {"row_0": other // CORES, "row_1": other % CORES}

    def side_peer(offset):
        other, device = row_peer(offset // XH)
        side = (h + offset % XH) % XH
        return other, side, {**device, "col_1": side}

    barrier = pltpu.get_barrier_semaphore()

    def greet(device):
        pl.semaphore_signal(barrier, inc=1, device_id=device, device_id_type=MESH)

    take_lower = pltpu.make_async_copy(lower_hbm.at[r], lower, in_sem.at[0])
    take_diag = pltpu.make_async_copy(diag_hbm, diag, in_sem.at[1])
    near = [{"col_0": (z + 1) % Z}, {"col_0": (z + Z - 1) % Z}, {"col_1": 1 - h}]
    near += [{"row_0": (y + 1) % Y}, {"row_0": (y + Y - 1) % Y}, {"row_1": 1 - k}]
    near += [{"wave": 1 - w}]
    for device in near:
        greet(device)

    take_lower.start()
    take_diag.start()
    places = [(z + offset) % Z for offset in (4, 3, 5, 2, 6, 1, 7, 0)]
    local = [
        pltpu.make_async_copy(ancestor.at[places[d], w], abuf.at[d, w], a_loc.at[d])
        for d in range(Z)
    ]
    for copy in local:
        copy.start()
    take_lower.wait()
    take_diag.wait()
    normed = dot_first(diag[r], lower[...])
    slot = 2 * c
    for g in range(2):
        packed[g][slot] = normed[g * PART : (g + 1) * PART, :BLK]
        packed[g][slot + 1] = normed[g * PART : (g + 1) * PART, BLK:]

    pl.semaphore_wait(barrier, len(near))

    def pair_at(g, place, side):
        return packed[g].at[pl.ds(2 * (place * XH + side), 2)]

    trades = []
    for g in range(2):
        own_pair = pair_at(g, z, h)
        trade = remote(own_pair, own_pair, h_sem.at[2 * g], h_sem.at[2 * g + 1], col_1=1 - h)
        trade.start()
        trades.append(trade)

    a_copies = [
        remote(
            ancestor.at[places[d], 1 - w],
            abuf.at[d, w],
            a_send.at[d],
            a_recv.at[d],
            wave=1 - w,
        )
        for d in range(Z)
    ]
    z_up, z_down = (z + 1) % Z, (z + Z - 1) % Z

    def z_gather(step, own, g, up):
        side = h if own == 0 else 1 - h
        source = (z + Z - (step - 1)) % Z if up else (z + step - 1) % Z
        if step < 4:
            view = pair_at(g, source, side)
        else:
            view = packed[g].at[pl.ds(2 * (source * XH + side) + (0 if up else 1), 1)]
        send, recv = (zp_send, zp_recv) if up else (zm_send, zm_recv)
        slot_id = 4 * (step - 1) + 2 * own + g
        return remote(
            view, view, send.at[slot_id], recv.at[slot_id], col_0=z_up if up else z_down
        )

    own_block = r * COLS + c
    wanted = [8 * c + j for j in range(8)] + [row * COLS + c for row in range(ROWS)]

    def look(m, carry):
        block = pattern[r, m]
        found = [jnp.where(block == goal, m + 1, old) for goal, old in zip(wanted, carry[:16])]
        kept = [
            jnp.where(pattern[s, m] == own_block, 1, old) for s, old in enumerate(carry[16:])
        ]
        return tuple(found + kept)

    def look_up():
        looked = lax.fori_loop(0, 32, look, (jnp.int32(0),) * 24)
        for s in range(ROWS):
            held[s] = looked[16 + s]
        return looked

    gathers = {}
    for step in range(1, 5):
        if step == 1:
            pieces = ((0, 0), (0, 1), (1, 0), (1, 1))
        else:
            pieces = ((0, 0), (1, 0), (0, 1), (1, 1))
        for own, g in pieces:
            if step == 1 and own == 1:
                trades[g].wait_recv()
            for up in (True, False):
                if step > 1:
                    gathers[step - 1, own, g, up].wait_recv()
                copy = z_gather(step, own, g, up)
                copy.start()
                gathers[step, own, g, up] = copy
        if step <= 2:
            a_copies[step - 1].start()
        if step == 1:
            looked = look_up()
        if step == 2:
            for s in range(ROWS):
                block_out[s] = dot_first(diag[s], diag[s])

    def placed(found, g):
        value = packed[g][jnp.maximum(found - 1, 0)]
        return jnp.where(found > 0, value, jnp.zeros_like(value))

    def place(g):
        for own in range(2):
            for up in (True, False):
                gathers[4, own, g, up].wait_recv()
        for j in range(8):
            dense[g][0, :, j * BLK : (j + 1) * BLK] = placed(looked[j], g)

    def spot(item, dy, core):
        return (item * Y + dy) * CORES + core

    def spread(g, source, target, send, recv, **device):
        return remote(
            dense[g].at[spot(*source)], dense[g].at[spot(*target)], send, recv, **device
        )

    y_up, y_down = (y + 1) % Y, (y + Y - 1) % Y
    waves = (w, 1 - w)

    def y_copy(g, item, up):
        slot_id = 4 * g + 2 * item + (0 if up else 1)
        return spread(
            g,
            (item, 0, 0),
            (item, 3 if up else 1, 0),
            y_send.at[slot_id],
            y_recv.at[slot_id],
            row_0=y_up if up else y_down,
        )

    def core_copy(g, item, dy):
        slot_id = 8 * g + 4 * item + dy
        return spread(
            g, (item, dy, 0), (item, dy, 1), c_send.at[slot_id], c_recv.at[slot_id], row_1=1 - k
        )

    def far_copy(g, item, up):
        rows = pl.ds(0 if up else PART // 2, PART // 2)
        slot_id = 4 * g + 2 * item + (0 if up else 1)
        return remote(
            dense[g].at[spot(item, 3 if up else 1, 0), rows],
            dense[g].at[spot(item, 2, 0), rows],
            f_send.at[slot_id],
            f_recv.at[slot_id],
            row_0=y_up if up else y_down,
        )

    both = [(g, item) for g in range(2) for item in range(2)]
    wave_copies = [
        spread(g, (0, 0, 0), (1, 0, 0), w_sem.at[2 * g], w_sem.at[2 * g + 1], wave=1 - w)
        for g in range(2)
    ]
    y_copies = {(*at, up): y_copy(*at, up) for at in both for up in (True, False)}
    far_copies = {(*at, up): far_copy(*at, up) for at in both for up in (True, False)}
    core_copies = {(*at, dy): core_copy(*at, dy) for at in both for dy in range(Y)}

    order = (0, 1, 3, 2)
    groups = (range(0, 2), range(2, 4), range(4, 6), range(6, 8))

    def kind(unit):
        return unit // 2 % 2, unit // 4, unit % 2

    def start_y(g, item):
        y_copies[g, item, True].start()
        y_copies[g, item, False].start()
        core_copies[g, item, 0].start()

    def start_far(g, item):
        for up, dy in ((True, 3), (False, 1)):
            y_copies[g, item, up].wait_recv()
            far_copies[g, item, up].start()
            core_copies[g, item, dy].start()

    def end_far(g, item):
        for up in (True, False):
            far_copies[g, item, up].wait_recv()
        core_copies[g, item, 2].start()

    def split(g, item, dys):
        for dy in dys:
            core_copies[g, item, dy].wait_recv()
            for core in range(CORES):
                start = (2 * item + g) * 256 + order.index(dy) * W + core * PART
                high, low = halves(dense[g][spot(item, dy, core)])
                dense_hi[start : start + PART, :] = high
                dense_lo[start : start + PART, :] = low

    def split_ancestor(d):
        local[d].wait()
        a_copies[d].wait_recv()
        for side in range(WAVES):
            high, low = halves(abuf[d, side])
            a_hi[d, :, side * HALF : (side + 1) * HALF] = high
            a_lo[d, :, side * HALF : (side + 1) * HALF] = low

    def multiply(group, first, count):
        right_hi = a_hi[first : first + count].reshape(count * BLK, KCOLS)
        right_lo = a_lo[first : first + count].reshape(count * BLK, KCOLS)
        rows = slice(groups[group][0] * BLK, (groups[group][-1] + 1) * BLK)
        left_hi, left_lo = dense_hi[rows, :], dense_lo[rows, :]
        product = (
            dot_last(left_hi, right_lo) + dot_last(left_lo, right_hi)
        ) + dot_last(left_hi, right_hi)
        for d in range(count):
            part[first + d, rows, :] = product[:, d * BLK : (d + 1) * BLK]

    def rows_of(unit):
        return pl.ds(unit * BLK, BLK)

    def chain(t, unit, up):
        slot_id = 0 if t == 0 else (2 * t - 1 if up else 2 * t)
        send, recv, into = (up_send, up_recv, up_in) if up else (down_send, down_recv, down_in)
        return remote(
            part.at[slot_id, rows_of(unit)],
            into.at[t, rows_of(unit)],
            send.at[t, unit],
            recv.at[t, unit],
            col_0=z_up if up else z_down,
        )

    chains = []

    def send_on(t, unit, up):
        copy = chain(t, unit, up)
        copy.start()
        chains.append(copy)

    def first_step(group):
        for unit in groups[group]:
            send_on(0, unit, unit % 2 == 0)

    def next_step(group, t):
        for unit in groups[group]:
            for up in (True, False):
                if t > 1 or (unit % 2 == 0) == up:
                    chain(t - 1, unit, up).wait_recv()
                    slot_id = 2 * t - 1 if up else 2 * t
                    into = up_in if up else down_in
                    part[slot_id, rows_of(unit), :] = (
                        part[slot_id, rows_of(unit), :] + into[t - 1, rows_of(unit), :]
                    )
                send_on(t, unit, up)

    def cross_copy(unit):
        g, item, pair = kind(unit)
        return remote(
            summed.at[rows_of(unit)],
            cross_in.at[h, 2 * g + pair],
            x_send.at[unit],
            x_recv.at[h, 2 * g + pair],
            col_1=w,
            wave=waves[item],
        )

    def last_step(group):
        for unit in groups[group]:
            g, item, pair = kind(unit)
            chain(3, unit, True).wait_recv()
            chain(3, unit, False).wait_recv()
            summed[rows_of(unit), :] = (
                part[7, rows_of(unit), :] + up_in[3, rows_of(unit), :]
            ) + down_in[3, rows_of(unit), :]
            if item == 1:
                cross_copy(unit).start()
            else:

                @pl.when(h != w)
                def _():
                    cross_copy(unit).start()

                @pl.when(h == w)
                def _():
                    cross_in[h, 2 * g + pair] = summed[rows_of(unit), :]

    place(0)
    wave_copies[0].start()
    start_y(0, 0)
    place(1)
    wave_copies[1].start()
    start_y(1, 0)
    for row in range(ROWS):
        for g in range(2):
            row_blocks[row, g * PART : (g + 1) * PART, :] = placed(looked[8 + row], g)
    own_rows[r] = row_blocks[r]
    split_ancestor(0)
    split_ancestor(1)
    split(0, 0, (0,))
    start_far(0, 0)
    wave_copies[0].wait_recv()
    start_y(0, 1)
    a_copies[2].start()
    split(0, 0, (1, 3))
    start_far(1, 0)
    wave_copies[1].wait_recv()
    start_y(1, 1)
    for d in range(3, Z):
        a_copies[d].start()
    end_far(0, 0)
    split(1, 0, (0, 1, 3))
    split(0, 0, (2,))
    multiply(0, 0, 1)
    first_step(0)
    start_far(0, 1)
    end_far(1, 0)
    split_ancestor(2)
    multiply(0, 1, 2)
    split(1, 0, (2,))
    multiply(1, 0, 1)
    first_step(1)
    next_step(0, 1)
    multiply(1, 1, 2)
    start_far(1, 1)
    split(0, 1, (0, 1, 3))
    next_step(1, 1)
    end_far(0, 1)
    split(1, 1, (0, 1, 3))
    split(0, 1, (2,))
    multiply(2, 0, 1)
    first_step(2)
    multiply(2, 1, 2)
    end_far(1, 1)
    block_copies = []
    for offset in range(1, ROWS):
        other, device = row_peer(offset)
        copy = remote(
            row_blocks.at[other],
            own_rows.at[r],
            b_send.at[offset],
            b_recv.at[offset],
            **device,
        )
        copy.start()
        block_copies.append(copy)
    split(1, 1, (2,))
    multiply(3, 0, 1)
    first_step(3)
    next_step(2, 1)
    multiply(3, 1, 2)
    split_ancestor(3)
    split_ancestor(4)
    multiply(0, 3, 2)
    next_step(3, 1)
    next_step(0, 2)
    multiply(1, 3, 2)
    next_step(1, 2)
    multiply(2, 3, 2)
    next_step(2, 2)
    multiply(3, 3, 2)
    split_ancestor(5)
    split_ancestor(6)
    multiply(0, 5, 2)
    next_step(0, 3)
    next_step(3, 2)
    multiply(1, 5, 2)
    next_step(1, 3)
    multiply(2, 5, 2)
    next_step(2, 3)
    multiply(3, 5, 2)
    split_ancestor(7)
    multiply(0, 7, 1)
    multiply(1, 7, 1)
    next_step(3, 3)
    last_step(0)
    multiply(2, 7, 1)
    multiply(3, 7, 1)
    last_step(1)
    last_step(2)
    last_step(3)

    for copy in block_copies:
        copy.wait_recv()

    def sibling(dy, core):
        return ((y + dy) % Y) * CORES + (k if core == 0 else 1 - k)

    for g, pair in ((0, 0), (0, 1), (1, 0), (1, 1)):
        for side in range(XH):

            @pl.when(jnp.logical_not(jnp.logical_and(h == w, h == side)))
            def _():
                remote(
                    summed.at[rows_of(0)],
                    cross_in.at[side, 2 * g + pair],
                    x_send.at[0],
                    x_recv.at[side, 2 * g + pair],
                    col_1=1 - h,
                ).wait_recv()

        for index in range(2):
            for core in range(CORES):
                s = sibling(order[2 * pair + index], core)
                rows = slice((2 * index + core) * PART, (2 * index + core + 1) * PART)
                value = -(cross_in[0, 2 * g + pair, rows, :] + cross_in[1, 2 * g + pair, rows, :])
                value = jnp.where(held[s] > 0, value, jnp.zeros_like(value))
                panel_out[s, g * PART : (g + 1) * PART, :] = value

    for dy in range(Y):
        squares = []
        for core in range(CORES):
            s = sibling(dy, core)
            squares.append(dot_last(own_rows[s], panel_out[s], HIGHEST))
        update[(y + dy) % Y, :, :W] = jnp.where(k == 0, squares[0], squares[1])
        update[(y + dy) % Y, :, W:] = jnp.where(k == 0, squares[1], squares[0])

    def share(row, side):
        start = (row % CORES) * 32 + side * 16
        return pl.ds(pl.multiple_of(start, 16), 16)

    u_copies = []
    for offset in range(1, ROWS * XH):
        other, side, device = side_peer(offset)
        copy = remote(
            update.at[other // CORES, share(other, side)],
            row_in.at[offset],
            u_send.at[offset],
            u_recv.at[offset],
            **device,
        )
        copy.start()
        u_copies.append(copy)
    mine = share(r, h)
    partial = update[y, mine, :]
    for offset in range(1, ROWS * XH):
        u_copies[offset - 1].wait_recv()
        partial = partial + row_in[offset]
    col_in[0] = partial
    v_copies = []
    for offset in (4, 3, 5, 2, 6, 1, 7):
        copy = remote(
            col_in.at[0],
            col_in.at[offset],
            v_send.at[offset],
            v_recv.at[offset],
            col_0=(z + offset) % Z,
        )
        copy.start()
        v_copies.append(copy)
    for copy in v_copies:
        copy.wait_recv()
    whole = col_in[z]
    for owner in range(1, Z):
        whole = whole + col_in[(z + Z - owner) % Z]
    total[y, mine, :] = whole
    t_copies = []
    for offset in range(1, ROWS * XH):
        copy = remote(
            total.at[y, mine],
            total.at[y, mine],
            t_send.at[offset],
            t_recv.at[offset],
            **side_peer(offset)[2],
        )
        copy.start()
        t_copies.append(copy)
    for copy in t_copies:
        copy.wait_recv()
    for s in range(ROWS):
        lanes = slice((s % 2) * W, (s % 2 + 1) * W)
        block_out[s] = block_out[s] - total[s // 2, :, lanes]

    for copy in trades + wave_copies:
        copy.wait_send()
    for copy in gathers.values():
        copy.wait_send()
    for copy in a_copies:
        copy.wait_send()
    for copy in y_copies.values():
        copy.wait_send()
    for copy in core_copies.values():
        copy.wait_send()
    for copy in far_copies.values():
        copy.wait_send()
    for copy in chains + block_copies + u_copies + v_copies + t_copies:
        copy.wait_send()
    for unit in range(8):
        if kind(unit)[1] == 1:
            cross_copy(unit).wait_send()
        else:

            @pl.when(h != w)
            def _():
                cross_copy(unit).wait_send()


def per_device(lower_panel, diag_inverse, ancestor_inverse, pattern):
    ancestor = ancestor_inverse.reshape(Z, XH, BLK, HALF)
    vmem = pl.BlockSpec(memory_space=pltpu.VMEM)
    hbm = pl.BlockSpec(memory_space=pl.ANY)
    dma = pltpu.SemaphoreType.DMA
    sibs = WAVES * ROWS * W
    outs = (
        jax.ShapeDtypeStruct((ROWS, W, BLK), F32),
        jax.ShapeDtypeStruct((ROWS, W, W), F32),
    )
    return pl.pallas_call(
        kernel,
        out_shape=tuple(pltpu.VMEM(out.shape, out.dtype) for out in outs),
        in_specs=[pl.BlockSpec(memory_space=pltpu.SMEM), hbm, hbm, hbm],
        out_specs=(vmem, vmem),
        scratch_shapes=[
            pltpu.VMEM((W, 2 * BLK), F32),
            pltpu.VMEM((ROWS, W, W), F32),
            pltpu.VMEM((32, PART, BLK), F32),
            pltpu.VMEM((32, PART, BLK), F32),
            pltpu.VMEM((WAVES * ROWS, PART, KCOLS), F32),
            pltpu.VMEM((WAVES * ROWS, PART, KCOLS), F32),
            pltpu.VMEM((sibs, KCOLS), BF16),
            pltpu.VMEM((sibs, KCOLS), BF16),
            pltpu.VMEM((Z, WAVES, BLK, HALF), F32),
            pltpu.VMEM((Z, BLK, KCOLS), BF16),
            pltpu.VMEM((Z, BLK, KCOLS), BF16),
            pltpu.VMEM((Z, sibs, BLK), F32),
            pltpu.VMEM((4, sibs, BLK), F32),
            pltpu.VMEM((4, sibs, BLK), F32),
            pltpu.VMEM((sibs, BLK), F32),
            pltpu.VMEM((XH, Y, 2 * W, BLK), F32),
            pltpu.VMEM((ROWS, W, BLK), F32),
            pltpu.VMEM((ROWS, W, BLK), F32),
            pltpu.VMEM((Y, W, BLK), F32),
            pltpu.VMEM((ROWS * XH, 16, BLK), F32),
            pltpu.VMEM((Z, 16, BLK), F32),
            pltpu.VMEM((Y, W, BLK), F32),
            pltpu.SMEM((ROWS,), jnp.int32),
            dma((2,)),
            dma((Z,)),
            dma((Z,)),
            dma((Z,)),
            dma((4,)),
            dma((16,)),
            dma((16,)),
            dma((16,)),
            dma((16,)),
            dma((4,)),
            dma((8,)),
            dma((8,)),
            dma((8,)),
            dma((8,)),
            dma((16,)),
            dma((16,)),
            dma((ROWS,)),
            dma((ROWS,)),
            dma((4, 8)),
            dma((4, 8)),
            dma((4, 8)),
            dma((4, 8)),
            dma((8,)),
            dma((2, 4)),
            dma((ROWS * XH,)),
            dma((ROWS * XH,)),
            dma((Z,)),
            dma((Z,)),
            dma((ROWS * XH,)),
            dma((ROWS * XH,)),
        ],
        compiler_params=pltpu.CompilerParams(
            collective_id=0, has_side_effects=True, vmem_limit_bytes=60 * 1024 * 1024
        ),
        name="wave",
    )(pattern, lower_panel, diag_inverse, ancestor)


def solution(mesh):
    finer = Mesh(
        mesh.devices.reshape(Y, CORES, Z, XH, WAVES),
        ("row_0", "row_1", "col_0", "col_1", "wave"),
    )
    placed = (P("wave", None, COL), P("wave", None, None), P(ROW, COL_WAVE), P("wave", None))
    return jax.shard_map(
        per_device,
        mesh=finer,
        in_specs=placed,
        out_specs=(P("wave", None, ROW_COL), P("wave", None, None)),
        check_vma=False,
    )
```

```python
import jax
import jax.numpy as jnp
from jax import lax
from jax.experimental import pallas as pl
from jax.experimental.pallas import tpu as pltpu
from jax.sharding import Mesh
from jax.sharding import PartitionSpec as P

W = 64
BLK = 128
PART = 32
Y, CORES, Z, XH, WAVES = 4, 2, 8, 2, 2
ROWS = Y * CORES
COLS = Z * XH
KCOLS = 1024
HALF = KCOLS // 2
COL = ("col_0", "col_1")
ROW = ("row_0", "row_1")
ROW_COL = ("row_0", "row_1", "col_0", "col_1")
COL_WAVE = ("col_0", "col_1", "wave")
MESH = pl.DeviceIdType.MESH
HIGHEST = lax.Precision.HIGHEST
F32 = jnp.float32
BF16 = jnp.bfloat16


def remote(src, dst, send, recv, **device):
    return pltpu.make_async_remote_copy(
        src_ref=src,
        dst_ref=dst,
        send_sem=send,
        recv_sem=recv,
        device_id=device,
        device_id_type=MESH,
    )


def halves(value):
    high = value.astype(BF16)
    return high, (value - high.astype(F32)).astype(BF16)


def dot_last(left, right, precision=None):
    return lax.dot_general(
        left, right, (((1,), (1,)), ((), ())), precision=precision, preferred_element_type=F32
    )


def dot_first(left, right):
    return lax.dot_general(
        left, right, (((0,), (0,)), ((), ())), precision=HIGHEST, preferred_element_type=F32
    )


def kernel(
    pattern,
    lower_hbm,
    diag_hbm,
    ancestor,
    panel_out,
    block_out,
    lower,
    diag,
    packed_a,
    packed_b,
    dense_a,
    dense_b,
    dense_hi,
    dense_lo,
    abuf,
    a_hi,
    a_lo,
    part,
    up_in,
    down_in,
    summed,
    cross_in,
    row_blocks,
    own_rows,
    pass_rows,
    far_rows,
    update,
    row_in,
    col_in,
    total,
    held,
    in_sem,
    a_send,
    a_recv,
    a_loc,
    h_sem,
    zp_send,
    zp_recv,
    zm_send,
    zm_recv,
    w_sem,
    y_send,
    y_recv,
    f_send,
    f_recv,
    c_send,
    c_recv,
    b_send,
    b_recv,
    p_sem,
    up_send,
    up_recv,
    down_send,
    down_recv,
    x_send,
    x_recv,
    u_send,
    u_recv,
    v_send,
    v_recv,
    t_send,
    t_recv,
):
    y = lax.axis_index("row_0")
    k = lax.axis_index("row_1")
    z = lax.axis_index("col_0")
    h = lax.axis_index("col_1")
    w = lax.axis_index("wave")
    r = y * CORES + k
    c = z * XH + h
    packed, dense = (packed_a, packed_b), (dense_a, dense_b)

    def row_peer(offset):
        other = (r + offset) % ROWS
        return other, {"row_0": other // CORES, "row_1": other % CORES}

    def side_peer(offset):
        other, device = row_peer(offset // XH)
        side = (h + offset % XH) % XH
        return other, side, {**device, "col_1": side}

    barrier = pltpu.get_barrier_semaphore()

    def greet(device):
        pl.semaphore_signal(barrier, inc=1, device_id=device, device_id_type=MESH)

    take_lower = pltpu.make_async_copy(lower_hbm.at[r], lower, in_sem.at[0])
    take_diag = pltpu.make_async_copy(diag_hbm, diag, in_sem.at[1])
    near = [{"col_0": (z + 1) % Z}, {"col_0": (z + Z - 1) % Z}, {"col_1": 1 - h}]
    near += [{"row_0": (y + 1) % Y}, {"row_0": (y + Y - 1) % Y}, {"row_1": 1 - k}]
    near += [{"wave": 1 - w}]
    for device in near:
        greet(device)

    take_lower.start()
    take_diag.start()
    places = [(z + offset) % Z for offset in (4, 3, 5, 2, 6, 1, 7, 0)]
    local = [
        pltpu.make_async_copy(ancestor.at[places[d], w], abuf.at[d, w], a_loc.at[d])
        for d in range(Z)
    ]
    for copy in local:
        copy.start()
    take_lower.wait()
    take_diag.wait()
    normed = dot_first(diag[r], lower[...])
    slot = 2 * c
    for g in range(2):
        packed[g][slot] = normed[g * PART : (g + 1) * PART, :BLK]
        packed[g][slot + 1] = normed[g * PART : (g + 1) * PART, BLK:]

    pl.semaphore_wait(barrier, len(near))

    def pair_at(g, place, side):
        return packed[g].at[pl.ds(2 * (place * XH + side), 2)]

    trades = []
    for g in range(2):
        own_pair = pair_at(g, z, h)
        trade = remote(own_pair, own_pair, h_sem.at[2 * g], h_sem.at[2 * g + 1], col_1=1 - h)
        trade.start()
        trades.append(trade)

    a_copies = [
        remote(
            ancestor.at[places[d], 1 - w],
            abuf.at[d, w],
            a_send.at[d],
            a_recv.at[d],
            wave=1 - w,
        )
        for d in range(Z)
    ]
    z_up, z_down = (z + 1) % Z, (z + Z - 1) % Z

    def z_gather(step, own, g, up):
        side = h if own == 0 else 1 - h
        source = (z + Z - (step - 1)) % Z if up else (z + step - 1) % Z
        if step < 4:
            view = pair_at(g, source, side)
        else:
            view = packed[g].at[pl.ds(2 * (source * XH + side) + (0 if up else 1), 1)]
        send, recv = (zp_send, zp_recv) if up else (zm_send, zm_recv)
        slot_id = 4 * (step - 1) + 2 * own + g
        return remote(
            view, view, send.at[slot_id], recv.at[slot_id], col_0=z_up if up else z_down
        )

    own_block = r * COLS + c
    wanted = [8 * c + j for j in range(8)]
    for parity in (w, 1 - w):
        wanted += [row * COLS + z * XH + parity for row in range(ROWS)]

    def look(m, carry):
        block = pattern[r, m]
        found = [jnp.where(block == goal, m + 1, old) for goal, old in zip(wanted, carry[:24])]
        kept = [
            jnp.where(pattern[s, m] == own_block, 1, old) for s, old in enumerate(carry[24:])
        ]
        return tuple(found + kept)

    def look_up():
        looked = lax.fori_loop(0, 32, look, (jnp.int32(0),) * 32)
        for s in range(ROWS):
            held[s] = looked[24 + s]
        return looked

    gathers = {}
    for step in range(1, 5):
        if step == 1:
            pieces = ((0, 0), (0, 1), (1, 0), (1, 1))
        else:
            pieces = ((0, 0), (1, 0), (0, 1), (1, 1))
        for own, g in pieces:
            if step == 1 and own == 1:
                trades[g].wait_recv()
            for up in (True, False):
                if step > 1:
                    gathers[step - 1, own, g, up].wait_recv()
                copy = z_gather(step, own, g, up)
                copy.start()
                gathers[step, own, g, up] = copy
        if step <= 2:
            a_copies[step - 1].start()
        if step == 1:
            looked = look_up()
        if step == 2:
            for s in range(ROWS):
                block_out[s] = dot_first(diag[s], diag[s])

    def placed(found, g):
        value = packed[g][jnp.maximum(found - 1, 0)]
        return jnp.where(found > 0, value, jnp.zeros_like(value))

    def place(g):
        for own in range(2):
            for up in (True, False):
                gathers[4, own, g, up].wait_recv()
        for j in range(8):
            dense[g][0, :, j * BLK : (j + 1) * BLK] = placed(looked[j], g)

    def spot(item, dy, core):
        return (item * Y + dy) * CORES + core

    def spread(g, source, target, send, recv, **device):
        return remote(
            dense[g].at[spot(*source)], dense[g].at[spot(*target)], send, recv, **device
        )

    y_up, y_down = (y + 1) % Y, (y + Y - 1) % Y
    waves = (w, 1 - w)

    def y_copy(g, item, up):
        slot_id = 4 * g + 2 * item + (0 if up else 1)
        return spread(
            g,
            (item, 0, 0),
            (item, 3 if up else 1, 0),
            y_send.at[slot_id],
            y_recv.at[slot_id],
            row_0=y_up if up else y_down,
        )

    def core_copy(g, item, dy):
        slot_id = 8 * g + 4 * item + dy
        return spread(
            g, (item, dy, 0), (item, dy, 1), c_send.at[slot_id], c_recv.at[slot_id], row_1=1 - k
        )

    def far_copy(g, item, up):
        rows = pl.ds(0 if up else PART // 2, PART // 2)
        slot_id = 4 * g + 2 * item + (0 if up else 1)
        return remote(
            dense[g].at[spot(item, 3 if up else 1, 0), rows],
            dense[g].at[spot(item, 2, 0), rows],
            f_send.at[slot_id],
            f_recv.at[slot_id],
            row_0=y_up if up else y_down,
        )

    both = [(g, item) for g in range(2) for item in range(2)]
    wave_copies = [
        spread(g, (0, 0, 0), (1, 0, 0), w_sem.at[2 * g], w_sem.at[2 * g + 1], wave=1 - w)
        for g in range(2)
    ]
    y_copies = {(*at, up): y_copy(*at, up) for at in both for up in (True, False)}
    far_copies = {(*at, up): far_copy(*at, up) for at in both for up in (True, False)}
    core_copies = {(*at, dy): core_copy(*at, dy) for at in both for dy in range(Y)}

    order = (0, 1, 3, 2)
    groups = (range(0, 2), range(2, 4), range(4, 6), range(6, 8))

    def kind(unit):
        return unit // 2 % 2, unit // 4, unit % 2

    def start_y(g, item):
        y_copies[g, item, True].start()
        y_copies[g, item, False].start()
        core_copies[g, item, 0].start()

    def start_far(g, item):
        for up, dy in ((True, 3), (False, 1)):
            y_copies[g, item, up].wait_recv()
            far_copies[g, item, up].start()
            core_copies[g, item, dy].start()

    def end_far(g, item):
        for up in (True, False):
            far_copies[g, item, up].wait_recv()
        core_copies[g, item, 2].start()

    def split(g, item, dys):
        for dy in dys:
            core_copies[g, item, dy].wait_recv()
            for core in range(CORES):
                start = (2 * item + g) * 256 + order.index(dy) * W + core * PART
                high, low = halves(dense[g][spot(item, dy, core)])
                dense_hi[start : start + PART, :] = high
                dense_lo[start : start + PART, :] = low

    def split_ancestor(d):
        local[d].wait()
        a_copies[d].wait_recv()
        for side in range(WAVES):
            high, low = halves(abuf[d, side])
            a_hi[d, :, side * HALF : (side + 1) * HALF] = high
            a_lo[d, :, side * HALF : (side + 1) * HALF] = low

    def multiply(group, first, count):
        right_hi = a_hi[first : first + count].reshape(count * BLK, KCOLS)
        right_lo = a_lo[first : first + count].reshape(count * BLK, KCOLS)
        rows = slice(groups[group][0] * BLK, (groups[group][-1] + 1) * BLK)
        left_hi, left_lo = dense_hi[rows, :], dense_lo[rows, :]
        product = (
            dot_last(left_hi, right_lo) + dot_last(left_lo, right_hi)
        ) + dot_last(left_hi, right_hi)
        for d in range(count):
            part[first + d, rows, :] = product[:, d * BLK : (d + 1) * BLK]

    def rows_of(unit):
        return pl.ds(unit * BLK, BLK)

    def chain(t, unit, up):
        slot_id = 0 if t == 0 else (2 * t - 1 if up else 2 * t)
        send, recv, into = (up_send, up_recv, up_in) if up else (down_send, down_recv, down_in)
        return remote(
            part.at[slot_id, rows_of(unit)],
            into.at[t, rows_of(unit)],
            send.at[t, unit],
            recv.at[t, unit],
            col_0=z_up if up else z_down,
        )

    chains = []

    def send_on(t, unit, up):
        copy = chain(t, unit, up)
        copy.start()
        chains.append(copy)

    def first_step(group):
        for unit in groups[group]:
            send_on(0, unit, unit % 2 == 0)

    def next_step(group, t):
        for unit in groups[group]:
            for up in (True, False):
                if t > 1 or (unit % 2 == 0) == up:
                    chain(t - 1, unit, up).wait_recv()
                    slot_id = 2 * t - 1 if up else 2 * t
                    into = up_in if up else down_in
                    part[slot_id, rows_of(unit), :] = (
                        part[slot_id, rows_of(unit), :] + into[t - 1, rows_of(unit), :]
                    )
                send_on(t, unit, up)

    def cross_copy(unit):
        g, item, pair = kind(unit)
        return remote(
            summed.at[rows_of(unit)],
            cross_in.at[h, 2 * g + pair],
            x_send.at[unit],
            x_recv.at[h, 2 * g + pair],
            col_1=w,
            wave=waves[item],
        )

    def last_step(group):
        for unit in groups[group]:
            g, item, pair = kind(unit)
            chain(3, unit, True).wait_recv()
            chain(3, unit, False).wait_recv()
            summed[rows_of(unit), :] = (
                part[7, rows_of(unit), :] + up_in[3, rows_of(unit), :]
            ) + down_in[3, rows_of(unit), :]

    def start_cross(group):
        for unit in groups[group]:
            g, item, pair = kind(unit)
            if item == 1:
                cross_copy(unit).start()
            else:

                @pl.when(h != w)
                def _():
                    cross_copy(unit).start()

                @pl.when(h == w)
                def _():
                    cross_in[h, 2 * g + pair] = summed[rows_of(unit), :]

    def sibling(dy, core):
        return ((y + dy) % Y) * CORES + (k if core == 0 else 1 - k)

    def share(row, side):
        start = (row % CORES) * 32 + side * 16
        return pl.ds(pl.multiple_of(start, 16), 16)

    u_copies = {}

    def start_update(item):
        blocks = own_rows if item == 0 else far_rows
        for dy in range(Y):
            squares = []
            for core in range(CORES):
                start = item * 512 + order.index(dy) * W + core * PART
                value = jnp.concatenate(
                    [summed[start + g * 256 : start + g * 256 + PART, :] for g in range(2)], axis=0
                )
                squares.append(dot_last(blocks[sibling(dy, core)], value, HIGHEST))
            update[item, (y + dy) % Y, :, :W] = jnp.where(k == 0, squares[0], squares[1])
            update[item, (y + dy) % Y, :, W:] = jnp.where(k == 0, squares[1], squares[0])
        for offset in range(1 - item, ROWS * XH):
            other, side, device = side_peer(offset)
            if item == 1:
                device["wave"] = 1 - w
            slot_id = item * ROWS * XH + offset
            copy = remote(
                update.at[item, other // CORES, share(other, side)],
                row_in.at[slot_id],
                u_send.at[slot_id],
                u_recv.at[slot_id],
                **device,
            )
            copy.start()
            u_copies[slot_id] = copy

    place(0)
    wave_copies[0].start()
    start_y(0, 0)
    place(1)
    wave_copies[1].start()
    start_y(1, 0)
    for place_id in range(2 * ROWS):
        for g in range(2):
            row_blocks[place_id, g * PART : (g + 1) * PART, :] = placed(looked[8 + place_id], g)
    own_rows[r] = row_blocks[r]
    pass_rows[r] = row_blocks[ROWS + r]
    split_ancestor(0)
    split_ancestor(1)
    split(0, 0, (0,))
    start_far(0, 0)
    wave_copies[0].wait_recv()
    start_y(0, 1)
    a_copies[2].start()
    split(0, 0, (1, 3))
    start_far(1, 0)
    wave_copies[1].wait_recv()
    start_y(1, 1)
    for d in range(3, Z):
        a_copies[d].start()
    end_far(0, 0)
    split(1, 0, (0, 1, 3))
    split(0, 0, (2,))
    multiply(0, 0, 1)
    first_step(0)
    start_far(0, 1)
    end_far(1, 0)
    split_ancestor(2)
    multiply(0, 1, 2)
    split(1, 0, (2,))
    multiply(1, 0, 1)
    first_step(1)
    next_step(0, 1)
    multiply(1, 1, 2)
    start_far(1, 1)
    split(0, 1, (0, 1, 3))
    next_step(1, 1)
    end_far(0, 1)
    split(1, 1, (0, 1, 3))
    split(0, 1, (2,))
    multiply(2, 0, 1)
    first_step(2)
    multiply(2, 1, 2)
    end_far(1, 1)
    block_copies = []
    for kept, into in enumerate((own_rows, pass_rows)):
        for offset in range(1, ROWS):
            other, device = row_peer(offset)
            slot_id = kept * ROWS + offset
            copy = remote(
                row_blocks.at[kept * ROWS + other],
                into.at[r],
                b_send.at[slot_id],
                b_recv.at[slot_id],
                **device,
            )
            copy.start()
            block_copies.append(copy)
    split(1, 1, (2,))
    multiply(3, 0, 1)
    first_step(3)
    next_step(2, 1)
    multiply(3, 1, 2)
    split_ancestor(3)
    split_ancestor(4)
    multiply(0, 3, 2)
    next_step(3, 1)
    next_step(0, 2)
    multiply(1, 3, 2)
    next_step(1, 2)
    multiply(2, 3, 2)
    next_step(2, 2)
    multiply(3, 3, 2)
    split_ancestor(5)
    split_ancestor(6)
    for copy in block_copies:
        copy.wait_recv()
    pass_copy = remote(pass_rows, far_rows, p_sem.at[0], p_sem.at[1], wave=1 - w)
    pass_copy.start()
    multiply(0, 5, 2)
    next_step(0, 3)
    next_step(3, 2)
    multiply(1, 5, 2)
    next_step(1, 3)
    multiply(2, 5, 2)
    next_step(2, 3)
    multiply(3, 5, 2)
    split_ancestor(7)
    multiply(0, 7, 1)
    multiply(1, 7, 1)
    next_step(3, 3)
    last_step(0)
    start_cross(0)
    multiply(2, 7, 1)
    multiply(3, 7, 1)
    last_step(1)
    start_cross(1)
    start_update(0)
    last_step(2)
    last_step(3)
    pass_copy.wait_recv()
    start_update(1)
    start_cross(2)
    start_cross(3)

    mine = share(r, h)
    partial = update[0, y, mine, :]
    for slot_id, copy in u_copies.items():
        copy.wait_recv()
        partial = partial + row_in[slot_id]
    col_in[0] = partial
    v_copies = []
    for offset in (4, 3, 5, 2, 6, 1, 7):
        copy = remote(
            col_in.at[0],
            col_in.at[offset],
            v_send.at[offset],
            v_recv.at[offset],
            col_0=(z + offset) % Z,
        )
        copy.start()
        v_copies.append(copy)

    for g, pair in ((0, 0), (0, 1), (1, 0), (1, 1)):
        for side in range(XH):

            @pl.when(jnp.logical_not(jnp.logical_and(h == w, h == side)))
            def _():
                remote(
                    summed.at[rows_of(0)],
                    cross_in.at[side, 2 * g + pair],
                    x_send.at[0],
                    x_recv.at[side, 2 * g + pair],
                    col_1=1 - h,
                ).wait_recv()

        for index in range(2):
            for core in range(CORES):
                s = sibling(order[2 * pair + index], core)
                rows = slice((2 * index + core) * PART, (2 * index + core + 1) * PART)
                value = -(cross_in[0, 2 * g + pair, rows, :] + cross_in[1, 2 * g + pair, rows, :])
                value = jnp.where(held[s] > 0, value, jnp.zeros_like(value))
                panel_out[s, g * PART : (g + 1) * PART, :] = value

    for copy in v_copies:
        copy.wait_recv()
    whole = col_in[z]
    for owner in range(1, Z):
        whole = whole + col_in[(z + Z - owner) % Z]
    total[y, mine, :] = whole
    t_copies = []
    for offset in range(1, ROWS * XH):
        copy = remote(
            total.at[y, mine],
            total.at[y, mine],
            t_send.at[offset],
            t_recv.at[offset],
            **side_peer(offset)[2],
        )
        copy.start()
        t_copies.append(copy)
    for copy in t_copies:
        copy.wait_recv()
    for s in range(ROWS):
        lanes = slice((s % 2) * W, (s % 2 + 1) * W)
        block_out[s] = block_out[s] + total[s // 2, :, lanes]

    for copy in trades + wave_copies + [pass_copy] + list(u_copies.values()):
        copy.wait_send()
    for copy in gathers.values():
        copy.wait_send()
    for copy in a_copies:
        copy.wait_send()
    for copy in y_copies.values():
        copy.wait_send()
    for copy in core_copies.values():
        copy.wait_send()
    for copy in far_copies.values():
        copy.wait_send()
    for copy in chains + block_copies + v_copies + t_copies:
        copy.wait_send()
    for unit in range(8):
        if kind(unit)[1] == 1:
            cross_copy(unit).wait_send()
        else:

            @pl.when(h != w)
            def _():
                cross_copy(unit).wait_send()


def per_device(lower_panel, diag_inverse, ancestor_inverse, pattern):
    ancestor = ancestor_inverse.reshape(Z, XH, BLK, HALF)
    vmem = pl.BlockSpec(memory_space=pltpu.VMEM)
    hbm = pl.BlockSpec(memory_space=pl.ANY)
    dma = pltpu.SemaphoreType.DMA
    sibs = WAVES * ROWS * W
    outs = (
        jax.ShapeDtypeStruct((ROWS, W, BLK), F32),
        jax.ShapeDtypeStruct((ROWS, W, W), F32),
    )
    return pl.pallas_call(
        kernel,
        out_shape=tuple(pltpu.VMEM(out.shape, out.dtype) for out in outs),
        in_specs=[pl.BlockSpec(memory_space=pltpu.SMEM), hbm, hbm, hbm],
        out_specs=(vmem, vmem),
        scratch_shapes=[
            pltpu.VMEM((W, 2 * BLK), F32),
            pltpu.VMEM((ROWS, W, W), F32),
            pltpu.VMEM((32, PART, BLK), F32),
            pltpu.VMEM((32, PART, BLK), F32),
            pltpu.VMEM((WAVES * ROWS, PART, KCOLS), F32),
            pltpu.VMEM((WAVES * ROWS, PART, KCOLS), F32),
            pltpu.VMEM((sibs, KCOLS), BF16),
            pltpu.VMEM((sibs, KCOLS), BF16),
            pltpu.VMEM((Z, WAVES, BLK, HALF), F32),
            pltpu.VMEM((Z, BLK, KCOLS), BF16),
            pltpu.VMEM((Z, BLK, KCOLS), BF16),
            pltpu.VMEM((Z, sibs, BLK), F32),
            pltpu.VMEM((4, sibs, BLK), F32),
            pltpu.VMEM((4, sibs, BLK), F32),
            pltpu.VMEM((sibs, BLK), F32),
            pltpu.VMEM((XH, Y, 2 * W, BLK), F32),
            pltpu.VMEM((2 * ROWS, W, BLK), F32),
            pltpu.VMEM((ROWS, W, BLK), F32),
            pltpu.VMEM((ROWS, W, BLK), F32),
            pltpu.VMEM((ROWS, W, BLK), F32),
            pltpu.VMEM((WAVES, Y, W, BLK), F32),
            pltpu.VMEM((WAVES * ROWS * XH, 16, BLK), F32),
            pltpu.VMEM((Z, 16, BLK), F32),
            pltpu.VMEM((Y, W, BLK), F32),
            pltpu.SMEM((ROWS,), jnp.int32),
            dma((2,)),
            dma((Z,)),
            dma((Z,)),
            dma((Z,)),
            dma((4,)),
            dma((16,)),
            dma((16,)),
            dma((16,)),
            dma((16,)),
            dma((4,)),
            dma((8,)),
            dma((8,)),
            dma((8,)),
            dma((8,)),
            dma((16,)),
            dma((16,)),
            dma((2 * ROWS,)),
            dma((2 * ROWS,)),
            dma((2,)),
            dma((4, 8)),
            dma((4, 8)),
            dma((4, 8)),
            dma((4, 8)),
            dma((8,)),
            dma((2, 4)),
            dma((WAVES * ROWS * XH,)),
            dma((WAVES * ROWS * XH,)),
            dma((Z,)),
            dma((Z,)),
            dma((ROWS * XH,)),
            dma((ROWS * XH,)),
        ],
        compiler_params=pltpu.CompilerParams(
            collective_id=0, has_side_effects=True, vmem_limit_bytes=60 * 1024 * 1024
        ),
        name="wave",
    )(pattern, lower_panel, diag_inverse, ancestor)


def solution(mesh):
    finer = Mesh(
        mesh.devices.reshape(Y, CORES, Z, XH, WAVES),
        ("row_0", "row_1", "col_0", "col_1", "wave"),
    )
    placed = (P("wave", None, COL), P("wave", None, None), P(ROW, COL_WAVE), P("wave", None))
    return jax.shard_map(
        per_device,
        mesh=finer,
        in_specs=placed,
        out_specs=(P("wave", None, ROW_COL), P("wave", None, None)),
        check_vma=False,
    )
```

```python
import jax
import jax.numpy as jnp
from jax import lax
from jax.experimental import pallas as pl
from jax.experimental.pallas import tpu as pltpu
from jax.sharding import Mesh
from jax.sharding import PartitionSpec as P

W = 64
BLK = 128
PART = 32
Y, CORES, Z, XH, WAVES = 4, 2, 8, 2, 2
ROWS = Y * CORES
COLS = Z * XH
KCOLS = 1024
HALF = KCOLS // 2
COL = ("col_0", "col_1")
ROW = ("row_0", "row_1")
ROW_COL = ("row_0", "row_1", "col_0", "col_1")
COL_WAVE = ("col_0", "col_1", "wave")
MESH = pl.DeviceIdType.MESH
HIGHEST = lax.Precision.HIGHEST
F32 = jnp.float32
BF16 = jnp.bfloat16


def remote(src, dst, send, recv, **device):
    return pltpu.make_async_remote_copy(
        src_ref=src,
        dst_ref=dst,
        send_sem=send,
        recv_sem=recv,
        device_id=device,
        device_id_type=MESH,
    )


def halves(value):
    high = value.astype(BF16)
    return high, (value - high.astype(F32)).astype(BF16)


def dot_last(left, right, precision=None):
    return lax.dot_general(
        left, right, (((1,), (1,)), ((), ())), precision=precision, preferred_element_type=F32
    )


def dot_first(left, right):
    return lax.dot_general(
        left, right, (((0,), (0,)), ((), ())), precision=HIGHEST, preferred_element_type=F32
    )


def kernel(
    pattern,
    lower_hbm,
    diag_hbm,
    ancestor,
    panel_out,
    block_out,
    lower,
    diag,
    packed_a,
    packed_b,
    dense_a,
    dense_b,
    dense_hi,
    dense_lo,
    abuf,
    a_hi,
    a_lo,
    part,
    up_in,
    down_in,
    summed,
    cross_in,
    row_blocks,
    own_rows,
    pass_rows,
    far_rows,
    update,
    row_in,
    col_in,
    total,
    held,
    in_sem,
    a_send,
    a_recv,
    a_loc,
    h_sem,
    zp_send,
    zp_recv,
    zm_send,
    zm_recv,
    w_sem,
    y_send,
    y_recv,
    f_send,
    f_recv,
    c_send,
    c_recv,
    b_send,
    b_recv,
    p_sem,
    up_send,
    up_recv,
    down_send,
    down_recv,
    x_send,
    x_recv,
    u_send,
    u_recv,
    v_send,
    v_recv,
    t_send,
    t_recv,
):
    y = lax.axis_index("row_0")
    k = lax.axis_index("row_1")
    z = lax.axis_index("col_0")
    h = lax.axis_index("col_1")
    w = lax.axis_index("wave")
    r = y * CORES + k
    c = z * XH + h
    packed, dense = (packed_a, packed_b), (dense_a, dense_b)

    def row_peer(offset):
        other = (r + offset) % ROWS
        return other, {"row_0": other // CORES, "row_1": other % CORES}

    def side_peer(offset):
        other, device = row_peer(offset // XH)
        side = (h + offset % XH) % XH
        return other, side, {**device, "col_1": side}

    barrier = pltpu.get_barrier_semaphore()

    def greet(device):
        pl.semaphore_signal(barrier, inc=1, device_id=device, device_id_type=MESH)

    take_lower = pltpu.make_async_copy(lower_hbm.at[r], lower, in_sem.at[0])
    take_diag = pltpu.make_async_copy(diag_hbm, diag, in_sem.at[1])
    near = [{"col_0": (z + 1) % Z}, {"col_0": (z + Z - 1) % Z}, {"col_1": 1 - h}]
    near += [{"row_0": (y + 1) % Y}, {"row_0": (y + Y - 1) % Y}, {"row_1": 1 - k}]
    near += [{"wave": 1 - w}]
    for device in near:
        greet(device)

    take_lower.start()
    take_diag.start()
    places = [(z + offset) % Z for offset in (4, 3, 5, 2, 6, 1, 7, 0)]
    local = [
        pltpu.make_async_copy(ancestor.at[places[d], w], abuf.at[d, w], a_loc.at[d])
        for d in range(Z)
    ]
    for copy in local:
        copy.start()
    take_lower.wait()
    take_diag.wait()
    normed = dot_first(diag[r], lower[...])
    slot = 2 * c
    for g in range(2):
        packed[g][slot] = normed[g * PART : (g + 1) * PART, :BLK]
        packed[g][slot + 1] = normed[g * PART : (g + 1) * PART, BLK:]

    pl.semaphore_wait(barrier, len(near))

    def pair_at(g, place, side):
        return packed[g].at[pl.ds(2 * (place * XH + side), 2)]

    trades = []
    for g in range(2):
        own_pair = pair_at(g, z, h)
        trade = remote(own_pair, own_pair, h_sem.at[2 * g], h_sem.at[2 * g + 1], col_1=1 - h)
        trade.start()
        trades.append(trade)

    a_copies = [
        remote(
            ancestor.at[places[d], 1 - w],
            abuf.at[d, w],
            a_send.at[d],
            a_recv.at[d],
            wave=1 - w,
        )
        for d in range(Z)
    ]
    z_up, z_down = (z + 1) % Z, (z + Z - 1) % Z

    def z_gather(step, own, g, up):
        side = h if own == 0 else 1 - h
        source = (z + Z - (step - 1)) % Z if up else (z + step - 1) % Z
        if step < 4:
            view = pair_at(g, source, side)
        else:
            view = packed[g].at[pl.ds(2 * (source * XH + side) + (0 if up else 1), 1)]
        send, recv = (zp_send, zp_recv) if up else (zm_send, zm_recv)
        slot_id = 4 * (step - 1) + 2 * own + g
        return remote(
            view, view, send.at[slot_id], recv.at[slot_id], col_0=z_up if up else z_down
        )

    own_block = r * COLS + c
    wanted = [8 * c + j for j in range(8)]
    for parity in (w, 1 - w):
        wanted += [row * COLS + z * XH + parity for row in range(ROWS)]

    def look(m, carry):
        block = pattern[r, m]
        found = [jnp.where(block == goal, m + 1, old) for goal, old in zip(wanted, carry[:24])]
        kept = [
            jnp.where(pattern[s, m] == own_block, 1, old) for s, old in enumerate(carry[24:])
        ]
        return tuple(found + kept)

    def look_up():
        looked = lax.fori_loop(0, 32, look, (jnp.int32(0),) * 32)
        for s in range(ROWS):
            held[s] = looked[24 + s]
        return looked

    gathers = {}
    for step in range(1, 5):
        if step == 1:
            pieces = ((0, 0), (0, 1), (1, 0), (1, 1))
        else:
            pieces = ((0, 0), (1, 0), (0, 1), (1, 1))
        for own, g in pieces:
            if step == 1 and own == 1:
                trades[g].wait_recv()
            for up in (True, False):
                if step > 1:
                    gathers[step - 1, own, g, up].wait_recv()
                copy = z_gather(step, own, g, up)
                copy.start()
                gathers[step, own, g, up] = copy
        if step <= 2:
            a_copies[step - 1].start()
        if step == 1:
            looked = look_up()
        if step == 2:
            for s in range(ROWS):
                block_out[s] = dot_first(diag[s], diag[s])

    def placed(found, g):
        value = packed[g][jnp.maximum(found - 1, 0)]
        return jnp.where(found > 0, value, jnp.zeros_like(value))

    def place(g):
        for own in range(2):
            for up in (True, False):
                gathers[4, own, g, up].wait_recv()
        for j in range(8):
            dense[g][0, :, j * BLK : (j + 1) * BLK] = placed(looked[j], g)

    def spot(item, dy, core):
        return (item * Y + dy) * CORES + core

    def spread(g, source, target, send, recv, **device):
        return remote(
            dense[g].at[spot(*source)], dense[g].at[spot(*target)], send, recv, **device
        )

    y_up, y_down = (y + 1) % Y, (y + Y - 1) % Y
    waves = (w, 1 - w)

    def y_copy(g, item, up):
        slot_id = 4 * g + 2 * item + (0 if up else 1)
        return spread(
            g,
            (item, 0, 0),
            (item, 3 if up else 1, 0),
            y_send.at[slot_id],
            y_recv.at[slot_id],
            row_0=y_up if up else y_down,
        )

    def core_copy(g, item, dy):
        slot_id = 8 * g + 4 * item + dy
        return spread(
            g, (item, dy, 0), (item, dy, 1), c_send.at[slot_id], c_recv.at[slot_id], row_1=1 - k
        )

    def far_copy(g, item, up):
        rows = pl.ds(0 if up else PART // 2, PART // 2)
        slot_id = 4 * g + 2 * item + (0 if up else 1)
        return remote(
            dense[g].at[spot(item, 3 if up else 1, 0), rows],
            dense[g].at[spot(item, 2, 0), rows],
            f_send.at[slot_id],
            f_recv.at[slot_id],
            row_0=y_up if up else y_down,
        )

    both = [(g, item) for g in range(2) for item in range(2)]
    wave_copies = [
        spread(g, (0, 0, 0), (1, 0, 0), w_sem.at[2 * g], w_sem.at[2 * g + 1], wave=1 - w)
        for g in range(2)
    ]
    y_copies = {(*at, up): y_copy(*at, up) for at in both for up in (True, False)}
    far_copies = {(*at, up): far_copy(*at, up) for at in both for up in (True, False)}
    core_copies = {(*at, dy): core_copy(*at, dy) for at in both for dy in range(Y)}

    order = (0, 1, 3, 2)
    groups = (range(0, 2), range(2, 4), range(4, 6), range(6, 8))

    def kind(unit):
        return unit % 2, unit // 4, unit // 2 % 2

    def first_row(g, item, dy, core):
        index = order.index(dy)
        return ((2 * item + index // 2) * 2 + g) * BLK + index % 2 * W + core * PART

    def start_y(g, item):
        y_copies[g, item, True].start()
        y_copies[g, item, False].start()
        core_copies[g, item, 0].start()

    def start_far(g, item):
        for up, dy in ((True, 3), (False, 1)):
            y_copies[g, item, up].wait_recv()
            far_copies[g, item, up].start()
            core_copies[g, item, dy].start()

    def end_far(g, item):
        for up in (True, False):
            far_copies[g, item, up].wait_recv()
        core_copies[g, item, 2].start()

    def split(g, item, dys):
        for dy in dys:
            core_copies[g, item, dy].wait_recv()
            for core in range(CORES):
                start = first_row(g, item, dy, core)
                high, low = halves(dense[g][spot(item, dy, core)])
                dense_hi[start : start + PART, :] = high
                dense_lo[start : start + PART, :] = low

    def split_ancestor(d):
        local[d].wait()
        a_copies[d].wait_recv()
        for side in range(WAVES):
            high, low = halves(abuf[d, side])
            a_hi[d, :, side * HALF : (side + 1) * HALF] = high
            a_lo[d, :, side * HALF : (side + 1) * HALF] = low

    def multiply(group, first, count):
        right_hi = a_hi[first : first + count].reshape(count * BLK, KCOLS)
        right_lo = a_lo[first : first + count].reshape(count * BLK, KCOLS)
        rows = slice(groups[group][0] * BLK, (groups[group][-1] + 1) * BLK)
        left_hi, left_lo = dense_hi[rows, :], dense_lo[rows, :]
        product = (
            dot_last(left_hi, right_lo) + dot_last(left_lo, right_hi)
        ) + dot_last(left_hi, right_hi)
        for d in range(count):
            part[first + d, rows, :] = product[:, d * BLK : (d + 1) * BLK]

    def rows_of(unit):
        return pl.ds(unit * BLK, BLK)

    def chain(t, unit, up):
        slot_id = 0 if t == 0 else (2 * t - 1 if up else 2 * t)
        send, recv, into = (up_send, up_recv, up_in) if up else (down_send, down_recv, down_in)
        return remote(
            part.at[slot_id, rows_of(unit)],
            into.at[t, rows_of(unit)],
            send.at[t, unit],
            recv.at[t, unit],
            col_0=z_up if up else z_down,
        )

    chains = []

    def send_on(t, unit, up):
        copy = chain(t, unit, up)
        copy.start()
        chains.append(copy)

    def first_step(group):
        for unit in groups[group]:
            send_on(0, unit, unit % 2 == 0)

    def next_step(group, t):
        for unit in groups[group]:
            for up in (True, False):
                if t > 1 or (unit % 2 == 0) == up:
                    chain(t - 1, unit, up).wait_recv()
                    slot_id = 2 * t - 1 if up else 2 * t
                    into = up_in if up else down_in
                    part[slot_id, rows_of(unit), :] = (
                        part[slot_id, rows_of(unit), :] + into[t - 1, rows_of(unit), :]
                    )
                send_on(t, unit, up)

    def cross_copy(unit):
        g, item, pair = kind(unit)
        return remote(
            summed.at[rows_of(unit)],
            cross_in.at[h, 2 * g + pair],
            x_send.at[unit],
            x_recv.at[h, 2 * g + pair],
            col_1=w,
            wave=waves[item],
        )

    def last_step(group):
        for unit in groups[group]:
            g, item, pair = kind(unit)
            chain(3, unit, True).wait_recv()
            chain(3, unit, False).wait_recv()
            summed[rows_of(unit), :] = (
                part[7, rows_of(unit), :] + up_in[3, rows_of(unit), :]
            ) + down_in[3, rows_of(unit), :]

    def start_cross(group):
        for unit in groups[group]:
            g, item, pair = kind(unit)
            if item == 1:
                cross_copy(unit).start()
            else:

                @pl.when(h != w)
                def _():
                    cross_copy(unit).start()

                @pl.when(h == w)
                def _():
                    cross_in[h, 2 * g + pair] = summed[rows_of(unit), :]

    def sibling(dy, core):
        return ((y + dy) % Y) * CORES + (k if core == 0 else 1 - k)

    def share(row, side):
        start = (row % CORES) * 32 + side * 16
        return pl.ds(pl.multiple_of(start, 16), 16)

    u_copies = {}

    def start_update(item):
        blocks = own_rows if item == 0 else far_rows
        for dy in range(Y):
            squares = []
            for core in range(CORES):
                starts = [first_row(g, item, dy, core) for g in range(2)]
                value = jnp.concatenate(
                    [summed[start : start + PART, :] for start in starts], axis=0
                )
                squares.append(dot_last(blocks[sibling(dy, core)], value, HIGHEST))
            update[item, (y + dy) % Y, :, :W] = jnp.where(k == 0, squares[0], squares[1])
            update[item, (y + dy) % Y, :, W:] = jnp.where(k == 0, squares[1], squares[0])
        for offset in range(1 - item, ROWS * XH):
            other, side, device = side_peer(offset)
            if item == 1:
                device["wave"] = 1 - w
            slot_id = item * ROWS * XH + offset
            copy = remote(
                update.at[item, other // CORES, share(other, side)],
                row_in.at[slot_id],
                u_send.at[slot_id],
                u_recv.at[slot_id],
                **device,
            )
            copy.start()
            u_copies[slot_id] = copy

    place(0)
    wave_copies[0].start()
    start_y(0, 0)
    place(1)
    wave_copies[1].start()
    start_y(1, 0)
    for place_id in range(2 * ROWS):
        for g in range(2):
            row_blocks[place_id, g * PART : (g + 1) * PART, :] = placed(looked[8 + place_id], g)
    own_rows[r] = row_blocks[r]
    pass_rows[r] = row_blocks[ROWS + r]
    split_ancestor(0)
    split_ancestor(1)
    split(0, 0, (0,))
    start_far(0, 0)
    a_copies[2].start()
    start_far(1, 0)
    for d in range(3, Z):
        a_copies[d].start()
    split(0, 0, (1,))
    split(1, 0, (0, 1))
    multiply(0, 0, 1)
    first_step(0)
    wave_copies[0].wait_recv()
    start_y(0, 1)
    wave_copies[1].wait_recv()
    start_y(1, 1)
    end_far(0, 0)
    end_far(1, 0)
    for g in range(2):
        split(g, 0, (3, 2))
    multiply(1, 0, 1)
    first_step(1)
    start_far(0, 1)
    split_ancestor(2)
    multiply(0, 1, 2)
    next_step(0, 1)
    multiply(1, 1, 2)
    start_far(1, 1)
    next_step(1, 1)
    for g in range(2):
        split(g, 1, (0, 1))
    multiply(2, 0, 1)
    first_step(2)
    multiply(2, 1, 2)
    end_far(0, 1)
    end_far(1, 1)
    block_copies = []
    for kept, into in enumerate((own_rows, pass_rows)):
        for offset in range(1, ROWS):
            other, device = row_peer(offset)
            slot_id = kept * ROWS + offset
            copy = remote(
                row_blocks.at[kept * ROWS + other],
                into.at[r],
                b_send.at[slot_id],
                b_recv.at[slot_id],
                **device,
            )
            copy.start()
            block_copies.append(copy)
    for g in range(2):
        split(g, 1, (3, 2))
    multiply(3, 0, 1)
    first_step(3)
    next_step(2, 1)
    multiply(3, 1, 2)
    split_ancestor(3)
    split_ancestor(4)
    multiply(0, 3, 2)
    next_step(3, 1)
    next_step(0, 2)
    multiply(1, 3, 2)
    next_step(1, 2)
    multiply(2, 3, 2)
    next_step(2, 2)
    multiply(3, 3, 2)
    split_ancestor(5)
    split_ancestor(6)
    for copy in block_copies:
        copy.wait_recv()
    pass_copy = remote(pass_rows, far_rows, p_sem.at[0], p_sem.at[1], wave=1 - w)
    pass_copy.start()
    multiply(0, 5, 2)
    next_step(0, 3)
    next_step(3, 2)
    multiply(1, 5, 2)
    next_step(1, 3)
    multiply(2, 5, 2)
    next_step(2, 3)
    multiply(3, 5, 2)
    split_ancestor(7)
    multiply(0, 7, 1)
    multiply(1, 7, 1)
    next_step(3, 3)
    last_step(0)
    start_cross(0)
    multiply(2, 7, 1)
    multiply(3, 7, 1)
    last_step(1)
    start_cross(1)
    start_update(0)
    last_step(2)
    last_step(3)
    pass_copy.wait_recv()
    start_update(1)
    start_cross(2)
    start_cross(3)

    mine = share(r, h)
    partial = update[0, y, mine, :]
    for slot_id, copy in u_copies.items():
        copy.wait_recv()
        partial = partial + row_in[slot_id]
    col_in[0] = partial
    v_copies = []
    for offset in (4, 3, 5, 2, 6, 1, 7):
        copy = remote(
            col_in.at[0],
            col_in.at[offset],
            v_send.at[offset],
            v_recv.at[offset],
            col_0=(z + offset) % Z,
        )
        copy.start()
        v_copies.append(copy)

    for g, pair in ((0, 0), (0, 1), (1, 0), (1, 1)):
        for side in range(XH):

            @pl.when(jnp.logical_not(jnp.logical_and(h == w, h == side)))
            def _():
                remote(
                    summed.at[rows_of(0)],
                    cross_in.at[side, 2 * g + pair],
                    x_send.at[0],
                    x_recv.at[side, 2 * g + pair],
                    col_1=1 - h,
                ).wait_recv()

        for index in range(2):
            for core in range(CORES):
                s = sibling(order[2 * pair + index], core)
                rows = slice((2 * index + core) * PART, (2 * index + core + 1) * PART)
                value = -(cross_in[0, 2 * g + pair, rows, :] + cross_in[1, 2 * g + pair, rows, :])
                value = jnp.where(held[s] > 0, value, jnp.zeros_like(value))
                panel_out[s, g * PART : (g + 1) * PART, :] = value

    for copy in v_copies:
        copy.wait_recv()
    whole = col_in[z]
    for owner in range(1, Z):
        whole = whole + col_in[(z + Z - owner) % Z]
    total[y, mine, :] = whole
    t_copies = []
    for offset in range(1, ROWS * XH):
        copy = remote(
            total.at[y, mine],
            total.at[y, mine],
            t_send.at[offset],
            t_recv.at[offset],
            **side_peer(offset)[2],
        )
        copy.start()
        t_copies.append(copy)
    for copy in t_copies:
        copy.wait_recv()
    for s in range(ROWS):
        lanes = slice((s % 2) * W, (s % 2 + 1) * W)
        block_out[s] = block_out[s] + total[s // 2, :, lanes]

    for copy in trades + wave_copies + [pass_copy] + list(u_copies.values()):
        copy.wait_send()
    for copy in gathers.values():
        copy.wait_send()
    for copy in a_copies:
        copy.wait_send()
    for copy in y_copies.values():
        copy.wait_send()
    for copy in core_copies.values():
        copy.wait_send()
    for copy in far_copies.values():
        copy.wait_send()
    for copy in chains + block_copies + v_copies + t_copies:
        copy.wait_send()
    for unit in range(8):
        if kind(unit)[1] == 1:
            cross_copy(unit).wait_send()
        else:

            @pl.when(h != w)
            def _():
                cross_copy(unit).wait_send()


def per_device(lower_panel, diag_inverse, ancestor_inverse, pattern):
    ancestor = ancestor_inverse.reshape(Z, XH, BLK, HALF)
    vmem = pl.BlockSpec(memory_space=pltpu.VMEM)
    hbm = pl.BlockSpec(memory_space=pl.ANY)
    dma = pltpu.SemaphoreType.DMA
    sibs = WAVES * ROWS * W
    outs = (
        jax.ShapeDtypeStruct((ROWS, W, BLK), F32),
        jax.ShapeDtypeStruct((ROWS, W, W), F32),
    )
    return pl.pallas_call(
        kernel,
        out_shape=tuple(pltpu.VMEM(out.shape, out.dtype) for out in outs),
        in_specs=[pl.BlockSpec(memory_space=pltpu.SMEM), hbm, hbm, hbm],
        out_specs=(vmem, vmem),
        scratch_shapes=[
            pltpu.VMEM((W, 2 * BLK), F32),
            pltpu.VMEM((ROWS, W, W), F32),
            pltpu.VMEM((32, PART, BLK), F32),
            pltpu.VMEM((32, PART, BLK), F32),
            pltpu.VMEM((WAVES * ROWS, PART, KCOLS), F32),
            pltpu.VMEM((WAVES * ROWS, PART, KCOLS), F32),
            pltpu.VMEM((sibs, KCOLS), BF16),
            pltpu.VMEM((sibs, KCOLS), BF16),
            pltpu.VMEM((Z, WAVES, BLK, HALF), F32),
            pltpu.VMEM((Z, BLK, KCOLS), BF16),
            pltpu.VMEM((Z, BLK, KCOLS), BF16),
            pltpu.VMEM((Z, sibs, BLK), F32),
            pltpu.VMEM((4, sibs, BLK), F32),
            pltpu.VMEM((4, sibs, BLK), F32),
            pltpu.VMEM((sibs, BLK), F32),
            pltpu.VMEM((XH, Y, 2 * W, BLK), F32),
            pltpu.VMEM((2 * ROWS, W, BLK), F32),
            pltpu.VMEM((ROWS, W, BLK), F32),
            pltpu.VMEM((ROWS, W, BLK), F32),
            pltpu.VMEM((ROWS, W, BLK), F32),
            pltpu.VMEM((WAVES, Y, W, BLK), F32),
            pltpu.VMEM((WAVES * ROWS * XH, 16, BLK), F32),
            pltpu.VMEM((Z, 16, BLK), F32),
            pltpu.VMEM((Y, W, BLK), F32),
            pltpu.SMEM((ROWS,), jnp.int32),
            dma((2,)),
            dma((Z,)),
            dma((Z,)),
            dma((Z,)),
            dma((4,)),
            dma((16,)),
            dma((16,)),
            dma((16,)),
            dma((16,)),
            dma((4,)),
            dma((8,)),
            dma((8,)),
            dma((8,)),
            dma((8,)),
            dma((16,)),
            dma((16,)),
            dma((2 * ROWS,)),
            dma((2 * ROWS,)),
            dma((2,)),
            dma((4, 8)),
            dma((4, 8)),
            dma((4, 8)),
            dma((4, 8)),
            dma((8,)),
            dma((2, 4)),
            dma((WAVES * ROWS * XH,)),
            dma((WAVES * ROWS * XH,)),
            dma((Z,)),
            dma((Z,)),
            dma((ROWS * XH,)),
            dma((ROWS * XH,)),
        ],
        compiler_params=pltpu.CompilerParams(
            collective_id=0, has_side_effects=True, vmem_limit_bytes=60 * 1024 * 1024
        ),
        name="wave",
    )(pattern, lower_panel, diag_inverse, ancestor)


def solution(mesh):
    finer = Mesh(
        mesh.devices.reshape(Y, CORES, Z, XH, WAVES),
        ("row_0", "row_1", "col_0", "col_1", "wave"),
    )
    placed = (P("wave", None, COL), P("wave", None, None), P(ROW, COL_WAVE), P("wave", None))
    return jax.shard_map(
        per_device,
        mesh=finer,
        in_specs=placed,
        out_specs=(P("wave", None, ROW_COL), P("wave", None, None)),
        check_vma=False,
    )
```

```python
import jax
import jax.numpy as jnp
from jax import lax
from jax.experimental import pallas as pl
from jax.experimental.pallas import tpu as pltpu
from jax.sharding import Mesh
from jax.sharding import PartitionSpec as P

W = 64
BLK = 128
PART = 32
Y, CORES, Z, XH, WAVES = 4, 2, 8, 2, 2
ROWS = Y * CORES
COLS = Z * XH
KCOLS = 1024
HALF = KCOLS // 2
COL = ("col_0", "col_1")
ROW = ("row_0", "row_1")
ROW_COL = ("row_0", "row_1", "col_0", "col_1")
COL_WAVE = ("col_0", "col_1", "wave")
MESH = pl.DeviceIdType.MESH
HIGHEST = lax.Precision.HIGHEST
F32 = jnp.float32
BF16 = jnp.bfloat16


def remote(src, dst, send, recv, **device):
    return pltpu.make_async_remote_copy(
        src_ref=src,
        dst_ref=dst,
        send_sem=send,
        recv_sem=recv,
        device_id=device,
        device_id_type=MESH,
    )


def halves(value):
    high = value.astype(BF16)
    return high, (value - high.astype(F32)).astype(BF16)


def dot_last(left, right, precision=None):
    return lax.dot_general(
        left, right, (((1,), (1,)), ((), ())), precision=precision, preferred_element_type=F32
    )


def dot_first(left, right):
    return lax.dot_general(
        left, right, (((0,), (0,)), ((), ())), precision=HIGHEST, preferred_element_type=F32
    )


def kernel(
    pattern,
    lower_hbm,
    diag_hbm,
    ancestor,
    panel_out,
    block_out,
    lower,
    diag,
    packed_a,
    packed_b,
    dense_a,
    dense_b,
    dense_hi,
    dense_lo,
    abuf,
    a_hi,
    a_lo,
    part,
    up_in,
    down_in,
    summed,
    cross_in,
    row_blocks,
    own_rows,
    pass_rows,
    far_rows,
    update,
    row_in,
    col_in,
    total,
    held,
    in_sem,
    a_send,
    a_recv,
    a_loc,
    h_sem,
    zp_send,
    zp_recv,
    zm_send,
    zm_recv,
    w_sem,
    y_send,
    y_recv,
    f_send,
    f_recv,
    c_send,
    c_recv,
    b_send,
    b_recv,
    p_sem,
    up_send,
    up_recv,
    down_send,
    down_recv,
    x_send,
    x_recv,
    u_send,
    u_recv,
    v_send,
    v_recv,
    t_send,
    t_recv,
):
    y = lax.axis_index("row_0")
    k = lax.axis_index("row_1")
    z = lax.axis_index("col_0")
    h = lax.axis_index("col_1")
    w = lax.axis_index("wave")
    r = y * CORES + k
    c = z * XH + h
    packed, dense = (packed_a, packed_b), (dense_a, dense_b)

    def row_peer(offset):
        other = (r + offset) % ROWS
        return other, {"row_0": other // CORES, "row_1": other % CORES}

    def side_peer(offset):
        other, device = row_peer(offset // XH)
        side = (h + offset % XH) % XH
        return other, side, {**device, "col_1": side}

    barrier = pltpu.get_barrier_semaphore()

    def greet(device):
        pl.semaphore_signal(barrier, inc=1, device_id=device, device_id_type=MESH)

    take_lower = pltpu.make_async_copy(lower_hbm.at[r], lower, in_sem.at[0])
    take_diag = pltpu.make_async_copy(diag_hbm, diag, in_sem.at[1])
    near = [{"col_0": (z + 1) % Z}, {"col_0": (z + Z - 1) % Z}, {"col_1": 1 - h}]
    near += [{"row_0": (y + 1) % Y}, {"row_0": (y + Y - 1) % Y}, {"row_1": 1 - k}]
    near += [{"wave": 1 - w}]
    for device in near:
        greet(device)

    take_lower.start()
    take_diag.start()
    places = [(z + offset) % Z for offset in (4, 3, 5, 2, 6, 1, 7, 0)]
    local = [
        pltpu.make_async_copy(ancestor.at[places[d], w], abuf.at[d, w], a_loc.at[d])
        for d in range(Z)
    ]
    for copy in local:
        copy.start()
    take_lower.wait()
    take_diag.wait()
    normed = dot_first(diag[r], lower[...])
    slot = 2 * c
    for g in range(2):
        packed[g][slot] = normed[g * PART : (g + 1) * PART, :BLK]
        packed[g][slot + 1] = normed[g * PART : (g + 1) * PART, BLK:]

    pl.semaphore_wait(barrier, len(near))

    def pair_at(g, place, side):
        return packed[g].at[pl.ds(2 * (place * XH + side), 2)]

    trades = []
    for g in range(2):
        own_pair = pair_at(g, z, h)
        trade = remote(own_pair, own_pair, h_sem.at[2 * g], h_sem.at[2 * g + 1], col_1=1 - h)
        trade.start()
        trades.append(trade)

    a_copies = [
        remote(
            ancestor.at[places[d], 1 - w],
            abuf.at[d, w],
            a_send.at[d],
            a_recv.at[d],
            wave=1 - w,
        )
        for d in range(Z)
    ]
    z_up, z_down = (z + 1) % Z, (z + Z - 1) % Z

    def z_gather(step, own, g, up):
        side = h if own == 0 else 1 - h
        source = (z + Z - (step - 1)) % Z if up else (z + step - 1) % Z
        if step < 4:
            view = pair_at(g, source, side)
        else:
            view = packed[g].at[pl.ds(2 * (source * XH + side) + (0 if up else 1), 1)]
        send, recv = (zp_send, zp_recv) if up else (zm_send, zm_recv)
        slot_id = 4 * (step - 1) + 2 * own + g
        return remote(
            view, view, send.at[slot_id], recv.at[slot_id], col_0=z_up if up else z_down
        )

    own_block = r * COLS + c
    wanted = [8 * c + j for j in range(8)]
    for parity in (w, 1 - w):
        wanted += [row * COLS + z * XH + parity for row in range(ROWS)]

    def look(m, carry):
        block = pattern[r, m]
        found = [jnp.where(block == goal, m + 1, old) for goal, old in zip(wanted, carry[:24])]
        kept = [
            jnp.where(pattern[s, m] == own_block, 1, old) for s, old in enumerate(carry[24:])
        ]
        return tuple(found + kept)

    def look_up():
        looked = lax.fori_loop(0, 32, look, (jnp.int32(0),) * 32)
        for s in range(ROWS):
            held[s] = looked[24 + s]
        return looked

    gathers = {}
    for step in range(1, 5):
        if step == 1:
            pieces = ((0, 0), (0, 1), (1, 0), (1, 1))
        else:
            pieces = ((0, 0), (1, 0), (0, 1), (1, 1))
        for own, g in pieces:
            if step == 1 and own == 1:
                trades[g].wait_recv()
            for up in (True, False):
                if step > 1:
                    gathers[step - 1, own, g, up].wait_recv()
                copy = z_gather(step, own, g, up)
                copy.start()
                gathers[step, own, g, up] = copy
        if step <= 2:
            a_copies[step - 1].start()
        if step == 1:
            looked = look_up()
        if step == 2:
            for s in range(ROWS):
                block_out[s] = dot_first(diag[s], diag[s])

    def placed(found, g):
        value = packed[g][jnp.maximum(found - 1, 0)]
        return jnp.where(found > 0, value, jnp.zeros_like(value))

    def place(g):
        for own in range(2):
            for up in (True, False):
                gathers[4, own, g, up].wait_recv()
        for j in range(8):
            dense[g][0, :, j * BLK : (j + 1) * BLK] = placed(looked[j], g)

    def spot(item, dy, core):
        return (item * Y + dy) * CORES + core

    def spread(g, source, target, send, recv, **device):
        return remote(
            dense[g].at[spot(*source)], dense[g].at[spot(*target)], send, recv, **device
        )

    y_up, y_down = (y + 1) % Y, (y + Y - 1) % Y
    waves = (w, 1 - w)

    def y_copy(g, item, up):
        slot_id = 4 * g + 2 * item + (0 if up else 1)
        return spread(
            g,
            (item, 0, 0),
            (item, 3 if up else 1, 0),
            y_send.at[slot_id],
            y_recv.at[slot_id],
            row_0=y_up if up else y_down,
        )

    def core_copy(g, item, dy):
        slot_id = 8 * g + 4 * item + dy
        return spread(
            g, (item, dy, 0), (item, dy, 1), c_send.at[slot_id], c_recv.at[slot_id], row_1=1 - k
        )

    def far_copy(g, item, up):
        rows = pl.ds(0 if up else PART // 2, PART // 2)
        slot_id = 4 * g + 2 * item + (0 if up else 1)
        return remote(
            dense[g].at[spot(item, 3 if up else 1, 0), rows],
            dense[g].at[spot(item, 2, 0), rows],
            f_send.at[slot_id],
            f_recv.at[slot_id],
            row_0=y_up if up else y_down,
        )

    both = [(g, item) for g in range(2) for item in range(2)]
    wave_copies = [
        spread(g, (0, 0, 0), (1, 0, 0), w_sem.at[2 * g], w_sem.at[2 * g + 1], wave=1 - w)
        for g in range(2)
    ]
    y_copies = {(*at, up): y_copy(*at, up) for at in both for up in (True, False)}
    far_copies = {(*at, up): far_copy(*at, up) for at in both for up in (True, False)}
    core_copies = {(*at, dy): core_copy(*at, dy) for at in both for dy in range(Y)}

    order = (0, 1, 3, 2)
    groups = (range(0, 2), range(2, 4), range(4, 6), range(6, 8))

    def kind(unit):
        return unit % 2, unit // 4, unit // 2 % 2

    def first_row(g, item, dy, core):
        index = order.index(dy)
        return ((2 * item + index // 2) * 2 + g) * BLK + index % 2 * W + core * PART

    def start_y(g, item):
        y_copies[g, item, True].start()
        y_copies[g, item, False].start()
        core_copies[g, item, 0].start()

    def start_far(g, item):
        for up, dy in ((True, 3), (False, 1)):
            y_copies[g, item, up].wait_recv()
            far_copies[g, item, up].start()
            core_copies[g, item, dy].start()

    def end_far(g, item):
        for up in (True, False):
            far_copies[g, item, up].wait_recv()
        core_copies[g, item, 2].start()

    def split(g, item, dys):
        for dy in dys:
            core_copies[g, item, dy].wait_recv()
            for core in range(CORES):
                start = first_row(g, item, dy, core)
                high, low = halves(dense[g][spot(item, dy, core)])
                dense_hi[start : start + PART, :] = high
                dense_lo[start : start + PART, :] = low

    def split_ancestor(d):
        local[d].wait()
        a_copies[d].wait_recv()
        for side in range(WAVES):
            high, low = halves(abuf[d, side])
            a_hi[d, :, side * HALF : (side + 1) * HALF] = high
            a_lo[d, :, side * HALF : (side + 1) * HALF] = low

    def multiply(group, first, count):
        right_hi = a_hi[first : first + count].reshape(count * BLK, KCOLS)
        right_lo = a_lo[first : first + count].reshape(count * BLK, KCOLS)
        rows = slice(groups[group][0] * BLK, (groups[group][-1] + 1) * BLK)
        left_hi, left_lo = dense_hi[rows, :], dense_lo[rows, :]
        product = (
            dot_last(left_hi, right_lo) + dot_last(left_lo, right_hi)
        ) + dot_last(left_hi, right_hi)
        for d in range(count):
            part[first + d, rows, :] = product[:, d * BLK : (d + 1) * BLK]

    def rows_of(unit):
        return pl.ds(unit * BLK, BLK)

    def chain(t, unit, up):
        slot_id = 0 if t == 0 else (2 * t - 1 if up else 2 * t)
        send, recv, into = (up_send, up_recv, up_in) if up else (down_send, down_recv, down_in)
        return remote(
            part.at[slot_id, rows_of(unit)],
            into.at[t, rows_of(unit)],
            send.at[t, unit],
            recv.at[t, unit],
            col_0=z_up if up else z_down,
        )

    chains = []

    def send_on(t, unit, up):
        copy = chain(t, unit, up)
        copy.start()
        chains.append(copy)

    def first_step(group):
        for unit in groups[group]:
            send_on(0, unit, unit % 2 == 0)

    def next_step(group, t):
        for unit in groups[group]:
            for up in (True, False):
                if t > 1 or (unit % 2 == 0) == up:
                    chain(t - 1, unit, up).wait_recv()
                    slot_id = 2 * t - 1 if up else 2 * t
                    into = up_in if up else down_in
                    part[slot_id, rows_of(unit), :] = (
                        part[slot_id, rows_of(unit), :] + into[t - 1, rows_of(unit), :]
                    )
                send_on(t, unit, up)

    def cross_copy(unit):
        g, item, pair = kind(unit)
        return remote(
            summed.at[rows_of(unit)],
            cross_in.at[h, 2 * g + pair],
            x_send.at[unit],
            x_recv.at[h, 2 * g + pair],
            col_1=w,
            wave=waves[item],
        )

    def last_step(group):
        for unit in groups[group]:
            g, item, pair = kind(unit)
            chain(3, unit, True).wait_recv()
            chain(3, unit, False).wait_recv()
            summed[rows_of(unit), :] = (
                part[7, rows_of(unit), :] + up_in[3, rows_of(unit), :]
            ) + down_in[3, rows_of(unit), :]

    def start_cross(group):
        for unit in groups[group]:
            g, item, pair = kind(unit)
            if item == 1:
                cross_copy(unit).start()
            else:

                @pl.when(h != w)
                def _():
                    cross_copy(unit).start()

                @pl.when(h == w)
                def _():
                    cross_in[h, 2 * g + pair] = summed[rows_of(unit), :]

    def sibling(dy, core):
        return ((y + dy) % Y) * CORES + (k if core == 0 else 1 - k)

    def share(row, side):
        start = (row % CORES) * 32 + side * 16
        return pl.ds(pl.multiple_of(start, 16), 16)

    u_copies = {}

    def start_update(item):
        blocks = own_rows if item == 0 else far_rows
        for dy in range(Y):
            squares = []
            for core in range(CORES):
                starts = [first_row(g, item, dy, core) for g in range(2)]
                value = jnp.concatenate(
                    [summed[start : start + PART, :] for start in starts], axis=0
                )
                squares.append(dot_last(blocks[sibling(dy, core)], value, HIGHEST))
            update[item, (y + dy) % Y, :, :W] = jnp.where(k == 0, squares[0], squares[1])
            update[item, (y + dy) % Y, :, W:] = jnp.where(k == 0, squares[1], squares[0])
        for offset in range(1 - item, ROWS * XH):
            other, side, device = side_peer(offset)
            if item == 1:
                device["wave"] = 1 - w
            slot_id = item * ROWS * XH + offset
            copy = remote(
                update.at[item, other // CORES, share(other, side)],
                row_in.at[slot_id],
                u_send.at[slot_id],
                u_recv.at[slot_id],
                **device,
            )
            copy.start()
            u_copies[slot_id] = copy

    place(0)
    wave_copies[0].start()
    start_y(0, 0)
    place(1)
    wave_copies[1].start()
    start_y(1, 0)
    for place_id in range(2 * ROWS):
        for g in range(2):
            row_blocks[place_id, g * PART : (g + 1) * PART, :] = placed(looked[8 + place_id], g)
    own_rows[r] = row_blocks[r]
    pass_rows[r] = row_blocks[ROWS + r]
    split_ancestor(0)
    split_ancestor(1)
    split(0, 0, (0,))
    a_copies[2].start()
    start_far(0, 0)
    for d in range(3, Z):
        a_copies[d].start()
    start_far(1, 0)
    split(0, 0, (1,))
    split(1, 0, (0, 1))
    multiply(0, 0, 1)
    first_step(0)
    wave_copies[0].wait_recv()
    start_y(0, 1)
    wave_copies[1].wait_recv()
    start_y(1, 1)
    end_far(0, 0)
    end_far(1, 0)
    for g in range(2):
        split(g, 0, (3, 2))
    multiply(1, 0, 1)
    first_step(1)
    start_far(0, 1)
    split_ancestor(2)
    multiply(0, 1, 2)
    next_step(0, 1)
    multiply(1, 1, 2)
    start_far(1, 1)
    next_step(1, 1)
    for g in range(2):
        split(g, 1, (0, 1))
    multiply(2, 0, 1)
    first_step(2)
    multiply(2, 1, 2)
    end_far(0, 1)
    end_far(1, 1)
    block_copies = []
    for kept, into in enumerate((own_rows, pass_rows)):
        for offset in range(1, ROWS):
            other, device = row_peer(offset)
            slot_id = kept * ROWS + offset
            copy = remote(
                row_blocks.at[kept * ROWS + other],
                into.at[r],
                b_send.at[slot_id],
                b_recv.at[slot_id],
                **device,
            )
            copy.start()
            block_copies.append(copy)
    for g in range(2):
        split(g, 1, (3, 2))
    multiply(3, 0, 1)
    first_step(3)
    next_step(2, 1)
    multiply(3, 1, 2)
    split_ancestor(3)
    split_ancestor(4)
    multiply(0, 3, 2)
    next_step(3, 1)
    next_step(0, 2)
    multiply(1, 3, 2)
    next_step(1, 2)
    multiply(2, 3, 2)
    next_step(2, 2)
    multiply(3, 3, 2)
    split_ancestor(5)
    split_ancestor(6)
    for copy in block_copies:
        copy.wait_recv()
    pass_copy = remote(pass_rows, far_rows, p_sem.at[0], p_sem.at[1], wave=1 - w)
    pass_copy.start()
    multiply(0, 5, 2)
    next_step(0, 3)
    next_step(3, 2)
    multiply(1, 5, 2)
    next_step(1, 3)
    multiply(2, 5, 2)
    next_step(2, 3)
    multiply(3, 5, 2)
    split_ancestor(7)
    multiply(0, 7, 1)
    multiply(1, 7, 1)
    next_step(3, 3)
    last_step(0)
    start_cross(0)
    multiply(2, 7, 1)
    multiply(3, 7, 1)
    last_step(1)
    start_cross(1)
    start_update(0)
    last_step(2)
    last_step(3)
    pass_copy.wait_recv()
    start_update(1)
    start_cross(2)
    start_cross(3)

    mine = share(r, h)
    partial = update[0, y, mine, :]
    for slot_id, copy in u_copies.items():
        copy.wait_recv()
        partial = partial + row_in[slot_id]
    col_in[0] = partial
    v_copies = []
    for offset in (4, 3, 5, 2, 6, 1, 7):
        copy = remote(
            col_in.at[0],
            col_in.at[offset],
            v_send.at[offset],
            v_recv.at[offset],
            col_0=(z + offset) % Z,
        )
        copy.start()
        v_copies.append(copy)

    for g, pair in ((0, 0), (0, 1), (1, 0), (1, 1)):
        for side in range(XH):

            @pl.when(jnp.logical_not(jnp.logical_and(h == w, h == side)))
            def _():
                remote(
                    summed.at[rows_of(0)],
                    cross_in.at[side, 2 * g + pair],
                    x_send.at[0],
                    x_recv.at[side, 2 * g + pair],
                    col_1=1 - h,
                ).wait_recv()

        for index in range(2):
            for core in range(CORES):
                s = sibling(order[2 * pair + index], core)
                rows = slice((2 * index + core) * PART, (2 * index + core + 1) * PART)
                value = -(cross_in[0, 2 * g + pair, rows, :] + cross_in[1, 2 * g + pair, rows, :])
                value = jnp.where(held[s] > 0, value, jnp.zeros_like(value))
                panel_out[s, g * PART : (g + 1) * PART, :] = value

    for copy in v_copies:
        copy.wait_recv()
    whole = col_in[z]
    for owner in range(1, Z):
        whole = whole + col_in[(z + Z - owner) % Z]
    total[y, mine, :] = whole
    t_copies = []
    for offset in range(1, ROWS * XH):
        copy = remote(
            total.at[y, mine],
            total.at[y, mine],
            t_send.at[offset],
            t_recv.at[offset],
            **side_peer(offset)[2],
        )
        copy.start()
        t_copies.append(copy)
    for copy in t_copies:
        copy.wait_recv()
    for s in range(ROWS):
        lanes = slice((s % 2) * W, (s % 2 + 1) * W)
        block_out[s] = block_out[s] + total[s // 2, :, lanes]

    for copy in trades + wave_copies + [pass_copy] + list(u_copies.values()):
        copy.wait_send()
    for copy in gathers.values():
        copy.wait_send()
    for copy in a_copies:
        copy.wait_send()
    for copy in y_copies.values():
        copy.wait_send()
    for copy in core_copies.values():
        copy.wait_send()
    for copy in far_copies.values():
        copy.wait_send()
    for copy in chains + block_copies + v_copies + t_copies:
        copy.wait_send()
    for unit in range(8):
        if kind(unit)[1] == 1:
            cross_copy(unit).wait_send()
        else:

            @pl.when(h != w)
            def _():
                cross_copy(unit).wait_send()


def per_device(lower_panel, diag_inverse, ancestor_inverse, pattern):
    ancestor = ancestor_inverse.reshape(Z, XH, BLK, HALF)
    vmem = pl.BlockSpec(memory_space=pltpu.VMEM)
    hbm = pl.BlockSpec(memory_space=pl.ANY)
    dma = pltpu.SemaphoreType.DMA
    sibs = WAVES * ROWS * W
    outs = (
        jax.ShapeDtypeStruct((ROWS, W, BLK), F32),
        jax.ShapeDtypeStruct((ROWS, W, W), F32),
    )
    return pl.pallas_call(
        kernel,
        out_shape=tuple(pltpu.VMEM(out.shape, out.dtype) for out in outs),
        in_specs=[pl.BlockSpec(memory_space=pltpu.SMEM), hbm, hbm, hbm],
        out_specs=(vmem, vmem),
        scratch_shapes=[
            pltpu.VMEM((W, 2 * BLK), F32),
            pltpu.VMEM((ROWS, W, W), F32),
            pltpu.VMEM((32, PART, BLK), F32),
            pltpu.VMEM((32, PART, BLK), F32),
            pltpu.VMEM((WAVES * ROWS, PART, KCOLS), F32),
            pltpu.VMEM((WAVES * ROWS, PART, KCOLS), F32),
            pltpu.VMEM((sibs, KCOLS), BF16),
            pltpu.VMEM((sibs, KCOLS), BF16),
            pltpu.VMEM((Z, WAVES, BLK, HALF), F32),
            pltpu.VMEM((Z, BLK, KCOLS), BF16),
            pltpu.VMEM((Z, BLK, KCOLS), BF16),
            pltpu.VMEM((Z, sibs, BLK), F32),
            pltpu.VMEM((4, sibs, BLK), F32),
            pltpu.VMEM((4, sibs, BLK), F32),
            pltpu.VMEM((sibs, BLK), F32),
            pltpu.VMEM((XH, Y, 2 * W, BLK), F32),
            pltpu.VMEM((2 * ROWS, W, BLK), F32),
            pltpu.VMEM((ROWS, W, BLK), F32),
            pltpu.VMEM((ROWS, W, BLK), F32),
            pltpu.VMEM((ROWS, W, BLK), F32),
            pltpu.VMEM((WAVES, Y, W, BLK), F32),
            pltpu.VMEM((WAVES * ROWS * XH, 16, BLK), F32),
            pltpu.VMEM((Z, 16, BLK), F32),
            pltpu.VMEM((Y, W, BLK), F32),
            pltpu.SMEM((ROWS,), jnp.int32),
            dma((2,)),
            dma((Z,)),
            dma((Z,)),
            dma((Z,)),
            dma((4,)),
            dma((16,)),
            dma((16,)),
            dma((16,)),
            dma((16,)),
            dma((4,)),
            dma((8,)),
            dma((8,)),
            dma((8,)),
            dma((8,)),
            dma((16,)),
            dma((16,)),
            dma((2 * ROWS,)),
            dma((2 * ROWS,)),
            dma((2,)),
            dma((4, 8)),
            dma((4, 8)),
            dma((4, 8)),
            dma((4, 8)),
            dma((8,)),
            dma((2, 4)),
            dma((WAVES * ROWS * XH,)),
            dma((WAVES * ROWS * XH,)),
            dma((Z,)),
            dma((Z,)),
            dma((ROWS * XH,)),
            dma((ROWS * XH,)),
        ],
        compiler_params=pltpu.CompilerParams(
            collective_id=0, has_side_effects=True, vmem_limit_bytes=60 * 1024 * 1024
        ),
        name="wave",
    )(pattern, lower_panel, diag_inverse, ancestor)


def solution(mesh):
    finer = Mesh(
        mesh.devices.reshape(Y, CORES, Z, XH, WAVES),
        ("row_0", "row_1", "col_0", "col_1", "wave"),
    )
    placed = (P("wave", None, COL), P("wave", None, None), P(ROW, COL_WAVE), P("wave", None))
    return jax.shard_map(
        per_device,
        mesh=finer,
        in_specs=placed,
        out_specs=(P("wave", None, ROW_COL), P("wave", None, None)),
        check_vma=False,
    )
```
